256 devices in a mesh: tm: 4 (over y_hi, core), height: 64 (over y_lo, z, x).
Axes of the slice: x: 4, y: 4 (y_hi: 2, y_lo: 2; y = y_hi * 2 + y_lo), z: 8, core: 2. Of those that a mesh axis runs over, the one named last changes fastest.
Arguments:
- clip: bfloat16 [16, 64, 128, 256], P('tm', 'height'), may hold values from -6 to 6
- conv_weight: bfloat16 [3, 3, 3, 256, 256], replicated, may hold values from -0.078125 to 0.078125
- down_weight: bfloat16 [3, 256, 256], replicated, may hold values from -0.21875 to 0.21875
- grad_out: bfloat16 [8, 64, 128, 256], P('tm', 'height'), may hold values from -6 to 6
Outputs:
- grad_input: bfloat16 [16, 64, 128, 256], P('tm', 'height')
- grad_conv: float32 [6912, 256], P('height', 'tm')
- grad_down: float32 [768, 256], P('height', 'tm')
The draws below stay inside these ranges and needn't reach their ends.
All inputs are finite; a program needn't handle non-finite values.
Results may differ from the reference program's by a relative error of at most 0.0051.
Values may be sent and summed in bfloat16 or wider, within the bound.
A program may use at most 128 MiB of HBM per device.

```python
import jax
import jax.numpy as jnp

C = 256
WIDTH = 128
ROWS = 64
CLIPS = 1
ALL_ROWS = 64
FRAMES = 16
OUT_FRAMES = 8


def levels(rng, extent, split, least, top_value):
    factor_of = 1.0
    for position, parts in split:
        heights = jax.random.uniform(jax.random.fold_in(jax.random.fold_in(rng, 6), position), (parts,), jnp.float32, least / len(split), top_value / len(split))
        factor_of = factor_of * jnp.repeat(jnp.exp(heights), extent[position] // parts).reshape((-1,) + (1,) * (len(extent) - 1 - position))
    return factor_of


def centred(key, dims, scale, reach, shards=(), held_as=jnp.bfloat16):
    gain = levels(key, dims, shards, -0.22, 0.18) if shards else 1.0
    array = jax.random.normal(key, dims, jnp.float32) * scale * gain
    return jnp.minimum(jnp.maximum(array, -reach), reach).astype(held_as)


def setup_inputs(seed: int = 0) -> dict:
    keys = jax.random.split(jax.random.key(seed), 5)
    return {
        "clip": centred(keys[0], (FRAMES, ALL_ROWS, WIDTH, C), 1.0, 6.0, ((0, 4), (1, 64))),
        "conv_weight": centred(keys[1], (3, 3, 3, C, C), (27 * C) ** -0.5, 0.078125),
        "down_weight": centred(keys[2], (3, C, C), (3 * C) ** -0.5, 0.21875),
        "grad_out": centred(keys[3], (OUT_FRAMES, ALL_ROWS, WIDTH, C), 1.0, 6.0, ((0, 4), (1, 64))),
    }


def silu_grad(value):
    sig = jax.nn.sigmoid(value)
    return sig * (1.0 + value * (1.0 - sig))

def spread_back(here, later, down_weight):
    chans = here.shape[-1]
    here_flat = here.reshape(-1, chans)
    later_flat = later.reshape(-1, chans)
    even = jnp.dot(later_flat, down_weight[0].T, preferred_element_type=jnp.float32) + jnp.dot(here_flat, down_weight[2].T, preferred_element_type=jnp.float32)
    odd = jnp.dot(later_flat, down_weight[1].T, preferred_element_type=jnp.float32)
    shape = here.shape
    stacked = jnp.stack([even.reshape(shape), odd.reshape(shape)], axis=1)
    return stacked.reshape((2 * shape[0],) + shape[1:]).astype(jnp.bfloat16)

def one_clip(clip, conv_weight, down_weight, grad_out):
    nframes, nrows, ncols, chans = clip.shape
    cells = nframes * nrows * ncols
    inputs = clip.astype(jnp.float32)
    act = jax.nn.silu(inputs).astype(jnp.bfloat16)
    act_pad = jnp.pad(act, ((2, 0), (1, 1), (1, 1), (0, 0)))
    conv = jnp.zeros((cells, chans), jnp.float32)
    for a in range(3):
        for b in range(3):
            patch = jnp.concatenate([act_pad[a:a + nframes, b:b + nrows, c:c + ncols] for c in range(3)], axis=-1).reshape(cells, 3 * chans)
            conv = conv + jnp.dot(patch, conv_weight[a, b].reshape(3 * chans, chans), preferred_element_type=jnp.float32)
    summed = (inputs + conv.reshape(clip.shape)).astype(jnp.bfloat16)
    later = jnp.concatenate([grad_out[1:], jnp.zeros_like(grad_out[:1])], axis=0)
    grad_sum = spread_back(grad_out, later, down_weight)
    half = grad_out.shape[0]
    sum_pad = jnp.pad(summed, ((2, 0), (0, 0), (0, 0), (0, 0)))
    out_flat = grad_out.reshape(-1, chans)
    down_terms = []
    for k in range(3):
        picked = sum_pad[k:k + 2 * half:2].reshape(-1, chans)
        down_terms.append(jnp.dot(picked.T, out_flat, preferred_element_type=jnp.float32))
    grad_down = jnp.concatenate(down_terms, axis=0)
    grad_pad = jnp.pad(grad_sum, ((0, 2), (1, 1), (1, 1), (0, 0)))
    grad_flat = grad_sum.reshape(cells, chans)
    grad_act = jnp.zeros((cells, chans), jnp.float32)
    conv_terms = []
    for a in range(3):
        for b in range(3):
            patch = jnp.concatenate([act_pad[a:a + nframes, b:b + nrows, c:c + ncols] for c in range(3)], axis=-1).reshape(cells, 3 * chans)
            conv_terms.append(jnp.dot(patch.T, grad_flat, preferred_element_type=jnp.float32))
            back = jnp.concatenate([grad_pad[2 - a:2 - a + nframes, 2 - b:2 - b + nrows, 2 - c:2 - c + ncols] for c in range(3)], axis=-1).reshape(cells, 3 * chans)
            flipped = jnp.transpose(conv_weight[a, b], (0, 2, 1)).reshape(3 * chans, chans)
            grad_act = grad_act + jnp.dot(back, flipped, preferred_element_type=jnp.float32)
    grad_conv = jnp.concatenate(conv_terms, axis=0)
    grad_input = (grad_sum.astype(jnp.float32) + grad_act.reshape(clip.shape) * silu_grad(inputs)).astype(jnp.bfloat16)
    return (grad_input, grad_conv, grad_down)

def reference(clip, conv_weight, down_weight, grad_out):
    inputs_list = []
    grad_conv = jnp.zeros((27 * C, C), jnp.float32)
    grad_down = jnp.zeros((3 * C, C), jnp.float32)
    for index in range(CLIPS):
        lower = index * ROWS
        piece_in, piece_conv, piece_down = one_clip(clip[:, lower:lower + ROWS], conv_weight, down_weight, grad_out[:, lower:lower + ROWS])
        inputs_list.append(piece_in)
        grad_conv = grad_conv + piece_conv
        grad_down = grad_down + piece_down
    return (jnp.concatenate(inputs_list, axis=1), grad_conv, grad_down)
```

```python
import jax
import jax.numpy as jnp
from jax import lax
from jax.experimental import pallas as pl
from jax.experimental.pallas import tpu as pltpu
from jax.sharding import PartitionSpec as P

MESH = pl.DeviceIdType.MESH
F32 = jnp.float32
BF16 = jnp.bfloat16
COLS = 128
CH = 256
SIZES = (112, 112, 112, 112, 64)
DOWN = 4
TAPS = (((0, 4), (13, 17)), ((4, 7), (17, 21)), ((7, 11), (21, 24)), ((11, 13), (24, 27)))


def nt(lhs, rhs):
    return lax.dot_general(lhs, rhs, (((1,), (1,)), ((), ())), preferred_element_type=F32)


def nn(lhs, rhs):
    return jnp.dot(lhs, rhs, preferred_element_type=F32)


def sigmoid(value):
    return 1.0 / (1.0 + jnp.exp(-value))


def shifted(value, row):
    before = jnp.where(row == 0, 0.0, pltpu.roll(value, 1, 0))
    after = jnp.where(row == COLS - 1, 0.0, pltpu.roll(value, COLS - 1, 0))
    return before, after


def kernel(clip, weight, down, gout, g_in, g_conv, g_down, *scratch):
    scratch = list(scratch)
    take = lambda n: [scratch.pop(0) for _ in range(n)]
    (wgt, dwn, cl, go, acts, act_t, gs, cb, acc, part, part_d) = take(11)
    (zt, ztd, zr, zrd) = take(4)
    bufs = [take(9) for _ in SIZES]
    (loc_sem, halo_s, halo_r, red_s, red_r, zs, zsd, zrs, zrds) = take(9)

    tm = lax.axis_index("tm")
    h = lax.axis_index("height")
    core = lax.rem(tm, 2)
    yh = lax.div(tm, 2)
    x = lax.rem(h, 4)
    z = lax.rem(lax.div(h, 4), 8)
    yl = lax.div(h, 32)
    y = yh * 2 + yl

    def dev(xx, yy, zz, cc):
        return (lax.div(yy, 2) * 2 + cc, lax.rem(yy, 2) * 32 + zz * 4 + xx)

    def near(dt, dh):
        return (lax.rem(tm + dt + 4, 4), lax.rem(h + dh + 64, 64))

    def first(d):
        return dev(lax.rem(x + (1 - core) * d, 4), lax.rem(y + core * d, 4), z, core)

    def second(d):
        return dev(lax.rem(x + core * d, 4), lax.rem(y + (1 - core) * d, 4), z, core)

    def remote(src, dst, send, recv, device):
        return pltpu.make_async_remote_copy(
            src_ref=src, dst_ref=dst, send_sem=send, recv_sem=recv, device_id=device, device_id_type=MESH
        )

    barrier = pltpu.get_barrier_semaphore()
    peers = [near(dt, dh) for dt in (-1, 1) for dh in (-1, 0, 1)] + [near(0, -1), near(0, 1)]
    peers += [first(d) for d in (1, 2, 3)] + [second(d) for d in (1, 2, 3)]
    peers += [dev(x, y, lax.rem(z + d, 8), c) for d in range(1, 8) for c in (0, 1)]
    for peer in peers:
        pl.semaphore_signal(barrier, inc=1, device_id=peer, device_id_type=MESH)

    loads = [
        pltpu.make_async_copy(clip.at[:, 0], cl.at[pl.ds(2, 4)], loc_sem.at[0]),
        pltpu.make_async_copy(gout.at[:, 0], go.at[1, pl.ds(0, 2)], loc_sem.at[1]),
        pltpu.make_async_copy(down, dwn, loc_sem.at[2]),
    ] + [pltpu.make_async_copy(weight.at[a], wgt.at[a], loc_sem.at[3 + a]) for a in range(3)]
    for load in loads:
        load.start()

    pl.semaphore_wait(barrier, len(peers))

    halo = [
        (gout.at[:, 0], go.at[0, pl.ds(0, 2)], near(0, 1), h < 63, h > 0),
        (gout.at[:, 0], go.at[2, pl.ds(0, 2)], near(0, -1), h > 0, h < 63),
        (gout.at[:, 0], go.at[0, pl.ds(2, 2)], near(-1, 1), (tm > 0) & (h < 63), (tm < 3) & (h > 0)),
        (gout.at[:, 0], go.at[2, pl.ds(2, 2)], near(-1, -1), (tm > 0) & (h > 0), (tm < 3) & (h < 63)),
        (gout.at[:, 0], go.at[1, pl.ds(2, 2)], near(-1, 0), tm > 0, tm < 3),
        (clip.at[pl.ds(2, 2), 0], cl.at[pl.ds(0, 2)], near(1, 0), tm < 3, tm > 0),
    ]
    copies = [remote(s, d, halo_s.at[i], halo_r.at[i], to) for i, (s, d, to, _, _) in enumerate(halo)]

    def when_start(i):
        @pl.when(halo[i][3])
        def _():
            copies[i].start()

    def when_recv(i):
        @pl.when(halo[i][4])
        def _():
            copies[i].wait_recv()

        @pl.when(jnp.logical_not(halo[i][4]))
        def _():
            dst = halo[i][1]
            dst[...] = jnp.zeros(dst.shape, BF16)

    for i in (5, 0, 1, 4, 2, 3):
        when_start(i)

    row = lax.broadcasted_iota(jnp.int32, (COLS, CH), 0)

    def act_frame(f, carry):
        value = cl[f].astype(F32)
        act = value * sigmoid(value)
        before, after = shifted(act, row)
        acts[0, f] = before.astype(BF16)
        acts[1, f] = act.astype(BF16)
        acts[2, f] = after.astype(BF16)
        return carry

    loads[0].wait()
    lax.fori_loop(2, 6, act_frame, 0)
    act_t[...] = acts[1, pl.ds(2, 4)].reshape(4 * COLS, CH).T
    when_recv(5)
    lax.fori_loop(0, 2, act_frame, 0)
    for a in range(3):
        loads[3 + a].wait()

    def conv_rows(b, carry):
        total = jnp.zeros((4 * COLS, CH), F32)
        for a in range(3):
            lhs = jnp.concatenate([acts[c, pl.ds(a, 4)].reshape(4 * COLS, CH) for c in range(3)], axis=1)
            total = total + nn(lhs, wgt[a, b].reshape(3 * CH, CH))
        own = cl[pl.ds(2, 4)].reshape(4 * COLS, CH).astype(F32)
        total = total + jnp.where(b == 1, own, 0.0)
        cb[b] = total.astype(BF16).reshape(4, COLS, CH)
        return carry

    lax.fori_loop(0, 3, conv_rows, 0)

    loads[1].wait()
    loads[2].wait()
    for i in range(5):
        when_recv(i)

    def grad_rows(r, carry):
        later = go[r, pl.ds(1, 3)].reshape(3 * COLS, CH)
        here = go[r, pl.ds(0, 3)].reshape(3 * COLS, CH)
        even = nt(later, dwn[0]) + nt(here, dwn[2])
        odd = nt(later, dwn[1])
        for v in range(3):
            for k, whole in ((0, even), (1, odd)):
                value = whole[v * COLS : (v + 1) * COLS]
                before, after = shifted(value, row)
                gs[0, r, 2 * v + k] = after.astype(BF16)
                gs[1, r, 2 * v + k] = value.astype(BF16)
                gs[2, r, 2 * v + k] = before.astype(BF16)
        return carry

    lax.fori_loop(0, 3, grad_rows, 0)

    for k, pairs in ((0, ((0, 1), (2, 2))), (1, ((1, 1), (3, 2))), (2, ((0, 0), (2, 1)))):
        lhs = jnp.concatenate([cb[b, t] for b in range(3) for t, _ in pairs], axis=0)
        rhs = jnp.concatenate([go[2 - b, u] for b in range(3) for _, u in pairs], axis=0)
        part_d[k * CH : (k + 1) * CH, :] = lax.dot_general(
            lhs, rhs, (((0,), (0,)), ((), ())), preferred_element_type=F32
        )

    def taps(c):
        def one(t, carry):
            a, b, s = lax.div(t, 9), lax.rem(lax.div(t, 3), 3), lax.rem(t, 3)
            rhs = gs[s, 2 - b, pl.ds(2 - a, 4)].reshape(4 * COLS, CH)
            part[pl.ds(pl.multiple_of(t * CH, CH), CH), :] = nn(act_t[...], rhs)
            return carry

        for lo, hi in TAPS[c]:
            lax.fori_loop(lo, hi, one, 0)

    def blocks(c, cc, put):
        def two(i, carry):
            l, pair = lax.div(i, 2), lax.rem(i, 2)
            if c == DOWN:
                for j in range(4):
                    base = pl.multiple_of(24 * (16 * l + 2 * (2 * j + cc) + pair), 8)
                    each(part_d, base, 16, 8, slice(16 * j, 16 * j + 16), l, pair)
            else:
                base = pl.multiple_of(216 * (16 * l + 2 * (2 * c + cc) + pair), 8)
                each(part, base, 112, 104, slice(0, 112), l, pair)
            return carry

        def each(src, base, size, skip, where, l, pair):
            for odd in range(2):
                value = src[pl.ds(base + skip * odd, size), :]
                xx = 2 * pair + odd
                for hi in range(2):
                    yy = 2 * hi + l
                    p = (1 - cc) * xx + cc * yy
                    q = (1 - cc) * yy + cc * xx
                    put(p, q, where, value[:, 128 * hi : 128 * hi + 128])

        lax.fori_loop(0, 4, two, 0)

    partner = dev(x, y, z, 1 - core)
    p0 = (1 - core) * x + core * y
    q0 = (1 - core) * y + core * x
    pn, pp, po = lax.rem(p0 + 1, 4), lax.rem(p0 + 3, 4), lax.rem(p0 + 2, 4)

    def message(c, i):
        s_, sr, b_, leg, dr, cs, cm, r_, rx = bufs[c]
        lo, hi = pl.ds(0, 2), pl.ds(2, 2)
        if i == 0:
            src, dst, to = s_, sr, partner
        elif i == 1:
            src, dst, to = b_.at[po, lo], leg.at[0], first(1)
        elif i == 2:
            src, dst, to = b_.at[po, hi], leg.at[1], first(3)
        elif i == 3:
            src, dst, to = b_.at[pn, hi], dr.at[0], first(1)
        elif i == 4:
            src, dst, to = b_.at[pp, lo], dr.at[1], first(3)
        elif i == 5:
            src, dst, to = cs.at[0], cm.at[0], first(1)
        elif i == 6:
            src, dst, to = cs.at[1], cm.at[1], first(3)
        else:
            d = i - 6
            src, dst, to = r_.at[lax.rem(q0 + d, 4)], rx.at[d - 1], second(d)
        return remote(src, dst, red_s.at[c, i], red_r.at[c, i], to)

    def hand_over(c):
        s_ = bufs[c][0]

        def put(p, q, where, value):
            s_[p, q, where] = value.astype(BF16)

        blocks(c, 1 - core, put)
        message(c, 0).start()

    def combine(c):
        sr, b_ = bufs[c][1], bufs[c][2]
        message(c, 0).wait_recv()

        def put(p, q, where, value):
            b_[p, q, where] = (value + sr[p, q, where].astype(F32)).astype(BF16)

        blocks(c, core, put)
        for i in (1, 2, 3, 4):
            message(c, i).start()

    def relay(c):
        _, _, b_, leg, _, cs, _, _, _ = bufs[c]
        message(c, 1).wait_recv()
        cs[0] = (b_[pn, pl.ds(0, 2)].astype(F32) + leg[0].astype(F32)).astype(BF16)
        message(c, 5).start()
        message(c, 2).wait_recv()
        cs[1] = (b_[pp, pl.ds(2, 2)].astype(F32) + leg[1].astype(F32)).astype(BF16)
        message(c, 6).start()

    def turn(c):
        _, _, b_, _, dr, _, cm, r_, _ = bufs[c]
        for i in (3, 4, 5, 6):
            message(c, i).wait_recv()
        for half in range(2):
            both = pl.ds(2 * half, 2)
            total = b_[p0, both].astype(F32) + cm[half].astype(F32) + dr[1 - half].astype(F32)
            r_[both] = total.astype(BF16)
        for i in (7, 8, 9):
            message(c, i).start()

    lane = lax.broadcasted_iota(jnp.int32, (64, 128), 1)

    def z_send(src, dst, keep, send, recv, to_z, k):
        own = (to_z == z) & (core == k)

        @pl.when(own)
        def _():
            dst.at[z][...] = src[...]

        @pl.when(jnp.logical_not(own))
        def _():
            remote(src, dst.at[z], send, recv.at[z], dev(x, y, to_z, k)).start()

    def z_wait(src, dst, send, recv, to_z, k):
        @pl.when(jnp.logical_not((to_z == z) & (core == k)))
        def _():
            remote(src, dst.at[z], send, recv.at[z], dev(x, y, to_z, k)).wait_send()

    def leave(c):
        r_, rx = bufs[c][7], bufs[c][8]
        for i in (7, 8, 9):
            message(c, i).wait_recv()
        total = r_[q0].astype(F32)
        for d in range(3):
            total = total + rx[d].astype(F32)
        if c == DOWN:
            ztd[...] = total.astype(BF16).reshape(4, 16, 128)
            for j in range(4):
                for k in range(2):
                    z_send(ztd.at[j], zrd, None, zsd.at[j, k], zrds, 2 * j + core, k)
        else:
            top, low = total[0:64], total[48:112]
            zt[c, 0] = jnp.where(lane < 64, top, pltpu.roll(low, 64, 1)).astype(BF16)
            zt[c, 1] = jnp.where(lane < 64, pltpu.roll(top, 64, 1), low).astype(BF16)
            for k in range(2):
                z_send(zt.at[c, k], zr, None, zs.at[c, k], zrs, 2 * c + core, k)

    def grad_act(b):
        def one(a, carry):
            total = acc[...]
            for s in range(3):
                total = total + nt(gs[s, 2 - b, pl.ds(2 - a, 4)].reshape(4 * COLS, CH), wgt[a, b, s])
            acc[...] = total
            return carry

        lax.fori_loop(0, 3, one, 0)

    acc[...] = jnp.zeros(acc.shape, F32)
    hand_over(DOWN)
    taps(0)
    hand_over(0)
    combine(DOWN)
    taps(1)
    hand_over(1)
    combine(0)
    relay(DOWN)
    taps(2)
    hand_over(2)
    combine(1)
    relay(0)
    turn(DOWN)
    taps(3)
    hand_over(3)
    combine(2)
    relay(1)
    turn(0)
    combine(3)
    leave(DOWN)
    grad_act(0)
    relay(2)
    turn(1)
    leave(0)
    grad_act(1)
    relay(3)
    turn(2)
    leave(1)
    grad_act(2)

    def finish(f, carry):
        value = cl[f + 2].astype(F32)
        sig = sigmoid(value)
        grad = acc[pl.ds(pl.multiple_of(f * COLS, COLS), COLS), :]
        g_in[f, 0] = (gs[1, 1, f].astype(F32) + grad * (sig * (1.0 + value * (1.0 - sig)))).astype(BF16)
        return carry

    lax.fori_loop(0, 4, finish, 0)
    turn(3)
    leave(2)
    leave(3)

    mine = lax.rem(z, 2)
    for s in range(8):
        @pl.when(jnp.logical_not((z == s) & (core == mine)))
        def _():
            remote(ztd.at[0], zrd.at[s], zsd.at[0, 0], zrds.at[s], partner).wait_recv()
            remote(zt.at[0, 0], zr.at[s], zs.at[0, 0], zrs.at[s], partner).wait_recv()

    x_odd = lax.rem(x, 2) == 1
    total = zr[0].astype(F32)
    total_d = zrd[0].astype(F32)
    for s in range(1, 8):
        total = total + zr[s].astype(F32)
        total_d = total_d + zrd[s].astype(F32)
    whole = jnp.concatenate([total, pltpu.roll(total, 64, 1)[16:64]], axis=0)
    whole = jnp.where(x_odd, pltpu.roll(whole, 108, 0), whole)
    g_conv[...] = whole[0:108, 0:64]
    total_d = jnp.where(core == 1, pltpu.roll(total_d, 64, 1), total_d)
    total_d = jnp.where(x_odd, pltpu.roll(total_d, 12, 0), total_d)
    g_down[...] = total_d[0:12, 0:64]

    for i in range(6):
        @pl.when(halo[i][3])
        def _():
            copies[i].wait_send()

    for c in range(5):
        for i in range(10):
            message(c, i).wait_send()
    for c in range(4):
        for k in range(2):
            z_wait(zt.at[c, k], zr, zs.at[c, k], zrs, 2 * c + core, k)
            z_wait(ztd.at[c], zrd, zsd.at[c, k], zrds, 2 * c + core, k)


def body(clip, weight, down, gout):
    vmem = pltpu.VMEM
    chunk = []
    for n in SIZES:
        full, pair = (4, 4, n, 128), (2, 2, n, 128)
        chunk += [vmem(s, BF16) for s in (full, full, full, pair, pair, pair, pair, (4, n, 128), (3, n, 128))]
    dma = pltpu.SemaphoreType.DMA
    scratch = [
        vmem((3, 3, 3, CH, CH), BF16),
        vmem((3, CH, CH), BF16),
        vmem((6, COLS, CH), BF16),
        vmem((3, 4, COLS, CH), BF16),
        vmem((3, 6, COLS, CH), BF16),
        vmem((CH, 4 * COLS), BF16),
        vmem((3, 3, 6, COLS, CH), BF16),
        vmem((3, 4, COLS, CH), BF16),
        vmem((4 * COLS, CH), F32),
        vmem((27 * CH, CH), F32),
        vmem((3 * CH, CH), F32),
        vmem((4, 2, 64, 128), BF16),
        vmem((4, 16, 128), BF16),
        vmem((8, 64, 128), BF16),
        vmem((8, 16, 128), BF16),
        *chunk,
        dma((6,)),
        dma((6,)),
        dma((6,)),
        dma((5, 10)),
        dma((5, 10)),
        dma((4, 2)),
        dma((4, 2)),
        dma((8,)),
        dma((8,)),
    ]
    return pl.pallas_call(
        kernel,
        out_shape=(
            jax.ShapeDtypeStruct(clip.shape, BF16),
            jax.ShapeDtypeStruct((108, 64), F32),
            jax.ShapeDtypeStruct((12, 64), F32),
        ),
        in_specs=[pl.BlockSpec(memory_space=pl.ANY)] * 4,
        out_specs=[pl.BlockSpec(memory_space=vmem)] * 3,
        scratch_shapes=scratch,
        compiler_params=pltpu.CompilerParams(collective_id=0, has_side_effects=True),
        name="block_backward",
    )(clip, weight, down, gout)


def solution(mesh):
    placed = (P("tm", "height", None, None), P(), P(), P("tm", "height", None, None))
    return jax.shard_map(
        body,
        mesh=mesh,
        in_specs=placed,
        out_specs=(P("tm", "height", None, None), P("height", "tm"), P("height", "tm")),
        check_vma=False,
    )
```

```python
import jax
import jax.numpy as jnp
from jax import lax
from jax.experimental import pallas as pl
from jax.experimental.pallas import tpu as pltpu
from jax.sharding import PartitionSpec as P

MESH = pl.DeviceIdType.MESH
F32 = jnp.float32
BF16 = jnp.bfloat16
COLS = 128
CH = 256
SIZES = (112, 112, 112, 112, 64)
DOWN = 4
OWN_ROW = (1, 3, 3)
TAPS = ((0, 5, 2), (2, 4, 2), (3, 0, 1), (8, 0, 1))


def nt(lhs, rhs):
    return lax.dot_general(lhs, rhs, (((1,), (1,)), ((), ())), preferred_element_type=F32)


def nn(lhs, rhs):
    return jnp.dot(lhs, rhs, preferred_element_type=F32)


def sigmoid(value):
    return 1.0 / (1.0 + jnp.exp(-value))


def shifted(value, row):
    before = jnp.where(row == 0, 0.0, pltpu.roll(value, 1, 0))
    after = jnp.where(row == COLS - 1, 0.0, pltpu.roll(value, COLS - 1, 0))
    return before, after


def kernel(clip, weight, down, gout, g_in, sums, *scratch):
    scratch = list(scratch)
    take = lambda n: [scratch.pop(0) for _ in range(n)]
    (wgt, dwn, cl, go, acts, act_t, gs, cb, acc, part, part_d, held) = take(12)
    (zt, ztd, zr, zrd) = take(4)
    bufs = [take(9) for _ in SIZES]
    (loc_sem, halo_s, halo_r, red_s, red_r, zs, zsd, zrs, zrds) = take(9)

    tm = lax.axis_index("tm")
    h = lax.axis_index("height")
    core = lax.rem(tm, 2)
    yh = lax.div(tm, 2)
    x = lax.rem(h, 4)
    z = lax.rem(lax.div(h, 4), 8)
    yl = lax.div(h, 32)
    y = yh * 2 + yl

    def dev(xx, yy, zz, cc):
        return (lax.div(yy, 2) * 2 + cc, lax.rem(yy, 2) * 32 + zz * 4 + xx)

    def near(dt, dh):
        return (lax.rem(tm + dt + 4, 4), lax.rem(h + dh + 64, 64))

    def first(d):
        return dev(lax.rem(x + (1 - core) * d, 4), lax.rem(y + core * d, 4), z, core)

    def second(d):
        return dev(lax.rem(x + core * d, 4), lax.rem(y + (1 - core) * d, 4), z, core)

    def remote(src, dst, send, recv, device):
        return pltpu.make_async_remote_copy(
            src_ref=src, dst_ref=dst, send_sem=send, recv_sem=recv, device_id=device, device_id_type=MESH
        )

    barrier = pltpu.get_barrier_semaphore()
    peers = [near(dt, dh) for dt in (-1, 1) for dh in (-1, 0, 1)] + [near(0, -1), near(0, 1)]
    peers += [first(d) for d in (1, 2, 3)] + [second(d) for d in (1, 2, 3)]
    peers += [dev(x, y, lax.rem(z + d, 8), c) for d in range(1, 8) for c in (0, 1)]
    for peer in peers:
        pl.semaphore_signal(barrier, inc=1, device_id=peer, device_id_type=MESH)

    loads = [
        pltpu.make_async_copy(clip.at[:, 0], cl.at[pl.ds(2, 4)], loc_sem.at[0]),
        pltpu.make_async_copy(gout.at[:, 0], go.at[1, pl.ds(0, 2)], loc_sem.at[1]),
        pltpu.make_async_copy(down, dwn, loc_sem.at[2]),
    ] + [pltpu.make_async_copy(weight.at[a], wgt.at[a], loc_sem.at[3 + a]) for a in range(3)]
    for load in loads:
        load.start()

    pl.semaphore_wait(barrier, len(peers))

    halo = [
        (gout.at[:, 0], go.at[0, pl.ds(0, 2)], near(0, 1), h < 63, h > 0),
        (gout.at[:, 0], go.at[2, pl.ds(0, 2)], near(0, -1), h > 0, h < 63),
        (gout.at[:, 0], go.at[0, pl.ds(2, 2)], near(-1, 1), (tm > 0) & (h < 63), (tm < 3) & (h > 0)),
        (gout.at[:, 0], go.at[2, pl.ds(2, 2)], near(-1, -1), (tm > 0) & (h > 0), (tm < 3) & (h < 63)),
        (gout.at[:, 0], go.at[1, pl.ds(2, 2)], near(-1, 0), tm > 0, tm < 3),
        (clip.at[pl.ds(2, 2), 0], cl.at[pl.ds(0, 2)], near(1, 0), tm < 3, tm > 0),
    ]
    copies = [remote(s, d, halo_s.at[i], halo_r.at[i], to) for i, (s, d, to, _, _) in enumerate(halo)]

    def when_start(i):
        @pl.when(halo[i][3])
        def _():
            copies[i].start()

    def when_recv(i):
        @pl.when(halo[i][4])
        def _():
            copies[i].wait_recv()

        @pl.when(jnp.logical_not(halo[i][4]))
        def _():
            dst = halo[i][1]
            dst[...] = jnp.zeros(dst.shape, BF16)

    for i in (5, 0, 1, 4, 2, 3):
        when_start(i)

    row = lax.broadcasted_iota(jnp.int32, (COLS, CH), 0)

    def act_frame(f, carry):
        value = cl[f].astype(F32)
        act = value * sigmoid(value)
        before, after = shifted(act, row)
        acts[0, f] = before.astype(BF16)
        acts[1, f] = act.astype(BF16)
        acts[2, f] = after.astype(BF16)
        return carry

    loads[0].wait()
    lax.fori_loop(2, 6, act_frame, 0)
    act_t[...] = acts[1, pl.ds(2, 4)].reshape(4 * COLS, CH).T
    when_recv(5)
    lax.fori_loop(0, 2, act_frame, 0)
    for a in range(3):
        loads[3 + a].wait()

    def conv_rows(b, carry):
        total = jnp.zeros((4 * COLS, CH), F32)
        for a in range(3):
            lhs = jnp.concatenate([acts[c, pl.ds(a, 4)].reshape(4 * COLS, CH) for c in range(3)], axis=1)
            total = total + nn(lhs, wgt[a, b].reshape(3 * CH, CH))
        own = cl[pl.ds(2, 4)].reshape(4 * COLS, CH).astype(F32)
        total = total + jnp.where(b == 1, own, 0.0)
        cb[b] = total.astype(BF16).reshape(4, COLS, CH)
        return carry

    lax.fori_loop(0, 3, conv_rows, 0)

    def grad_rows(r):
        later = go[r, pl.ds(1, 3)].reshape(3 * COLS, CH)
        here = go[r, pl.ds(0, 3)].reshape(3 * COLS, CH)
        even = nt(later, dwn[0]) + nt(here, dwn[2])
        odd = nt(later, dwn[1])
        for v in range(3):
            for k, whole in ((0, even), (1, odd)):
                value = whole[v * COLS : (v + 1) * COLS]
                before, after = shifted(value, row)
                gs[0, r, 2 * v + k] = after.astype(BF16)
                gs[1, r, 2 * v + k] = value.astype(BF16)
                gs[2, r, 2 * v + k] = before.astype(BF16)

    def down_terms():
        for k, pairs in ((0, ((0, 1), (2, 2))), (1, ((1, 1), (3, 2))), (2, ((0, 0), (2, 1)))):
            lhs = jnp.concatenate([cb[b, t] for b in range(3) for t, _ in pairs], axis=0)
            rhs = jnp.concatenate([go[2 - b, u] for b in range(3) for _, u in pairs], axis=0)
            part_d[k * CH : (k + 1) * CH, :] = lax.dot_general(
                lhs, rhs, (((0,), (0,)), ((), ())), preferred_element_type=F32
            )

    def taps(start, step, count):
        def one(i, carry):
            ab = start + step * i
            a, b = lax.div(ab, 3), lax.rem(ab, 3)
            for s in range(3):
                rhs = gs[s, 2 - b, pl.ds(2 - a, 4)].reshape(4 * COLS, CH)
                part[pl.ds(pl.multiple_of((3 * ab + s) * CH, CH), CH), :] = nn(act_t[...], rhs)
            return carry

        lax.fori_loop(0, count, one, 0)

    def blocks(c, cc, put):
        def two(i, carry):
            l, pair = lax.div(i, 2), lax.rem(i, 2)
            if c == DOWN:
                for j in range(4):
                    base = pl.multiple_of(24 * (16 * l + 2 * (2 * j + cc) + pair), 8)
                    each(part_d, base, 16, 8, slice(16 * j, 16 * j + 16), l, pair)
            else:
                base = pl.multiple_of(216 * (16 * l + 2 * (2 * c + cc) + pair), 8)
                each(part, base, 112, 104, slice(0, 112), l, pair)
            return carry

        def each(src, base, size, skip, where, l, pair):
            for odd in range(2):
                value = src[pl.ds(base + skip * odd, size), :]
                xx = 2 * pair + odd
                for hi in range(2):
                    yy = 2 * hi + l
                    p = (1 - cc) * xx + cc * yy
                    q = (1 - cc) * yy + cc * xx
                    put(p, q, where, value[:, 128 * hi : 128 * hi + 128])

        lax.fori_loop(0, 4, two, 0)

    partner = dev(x, y, z, 1 - core)
    p0 = (1 - core) * x + core * y
    q0 = (1 - core) * y + core * x
    pn, pp, po = lax.rem(p0 + 1, 4), lax.rem(p0 + 3, 4), lax.rem(p0 + 2, 4)

    def message(c, i):
        s_, sr, b_, leg, dr, cs, cm, r_, rx = bufs[c]
        lo, hi = pl.ds(0, 2), pl.ds(2, 2)
        if i == 0:
            src, dst, to = s_, sr, partner
        elif i == 1:
            src, dst, to = b_.at[po, lo], leg.at[0], first(1)
        elif i == 2:
            src, dst, to = b_.at[po, hi], leg.at[1], first(3)
        elif i == 3:
            src, dst, to = b_.at[pn, hi], dr.at[0], first(1)
        elif i == 4:
            src, dst, to = b_.at[pp, lo], dr.at[1], first(3)
        elif i == 5:
            src, dst, to = cs.at[0], cm.at[0], first(1)
        elif i == 6:
            src, dst, to = cs.at[1], cm.at[1], first(3)
        else:
            d = i - 6
            src, dst, to = r_.at[lax.rem(q0 + d, 4)], rx.at[d - 1], second(d)
        return remote(src, dst, red_s.at[c, i], red_r.at[c, i], to)

    def hand_over(c):
        s_ = bufs[c][0]

        def put(p, q, where, value):
            s_[p, q, where] = value.astype(BF16)

        blocks(c, 1 - core, put)
        message(c, 0).start()

    def combine(c):
        sr, b_ = bufs[c][1], bufs[c][2]
        message(c, 0).wait_recv()

        def put(p, q, where, value):
            b_[p, q, where] = (value + sr[p, q, where].astype(F32)).astype(BF16)

        blocks(c, core, put)
        for i in (1, 2, 3, 4):
            message(c, i).start()

    def relay(c):
        _, _, b_, leg, _, cs, _, _, _ = bufs[c]
        message(c, 1).wait_recv()
        cs[0] = (b_[pn, pl.ds(0, 2)].astype(F32) + leg[0].astype(F32)).astype(BF16)
        message(c, 5).start()
        message(c, 2).wait_recv()
        cs[1] = (b_[pp, pl.ds(2, 2)].astype(F32) + leg[1].astype(F32)).astype(BF16)
        message(c, 6).start()

    def turn(c):
        _, _, b_, _, dr, _, cm, r_, _ = bufs[c]
        for i in (3, 4, 5, 6):
            message(c, i).wait_recv()
        for half in range(2):
            both = pl.ds(2 * half, 2)
            total = b_[p0, both].astype(F32) + cm[half].astype(F32) + dr[1 - half].astype(F32)
            r_[both] = total.astype(r_.dtype)
        for i in (7, 8, 9):
            message(c, i).start()

    lane = lax.broadcasted_iota(jnp.int32, (64, 128), 1)

    def z_send(src, dst, keep, send, recv, to_z, k):
        own = (to_z == z) & (core == k)

        @pl.when(own)
        def _():
            dst.at[z][...] = src[...]

        @pl.when(jnp.logical_not(own))
        def _():
            remote(src, dst.at[z], send, recv.at[z], dev(x, y, to_z, k)).start()

    def z_wait(src, dst, send, recv, to_z, k):
        @pl.when(jnp.logical_not((to_z == z) & (core == k)))
        def _():
            remote(src, dst.at[z], send, recv.at[z], dev(x, y, to_z, k)).wait_send()

    def leave(c):
        r_, rx = bufs[c][7], bufs[c][8]
        for i in (7, 8, 9):
            message(c, i).wait_recv()
        total = r_[q0].astype(F32)
        for d in range(3):
            total = total + rx[d].astype(F32)
        if c == DOWN:
            ztd[...] = total.reshape(4, 16, 128)
            for j in range(4):
                for k in range(2):
                    z_send(ztd.at[j], zrd, None, zsd.at[j, k], zrds, 2 * j + core, k)
        else:
            top, low = total[0:64], total[48:112]
            zt[c, 0] = jnp.where(lane < 64, top, pltpu.roll(low, 64, 1)).astype(BF16)
            zt[c, 1] = jnp.where(lane < 64, pltpu.roll(top, 64, 1), low).astype(BF16)
            for k in range(2):
                z_send(zt.at[c, k], zr, None, zs.at[c, k], zrs, 2 * c + core, k)

    def grad_act(b, total):
        for a in range(3):
            for s in range(3):
                total = total + nt(gs[s, 2 - b, pl.ds(2 - a, 4)].reshape(4 * COLS, CH), wgt[a, b, s])
        return total

    def finish(f, carry):
        value = cl[f + 2].astype(F32)
        sig = sigmoid(value)
        grad = acc[pl.ds(pl.multiple_of(f * COLS, COLS), COLS), :]
        held[f, 0] = (gs[1, 1, f].astype(F32) + grad * (sig * (1.0 + value * (1.0 - sig)))).astype(BF16)
        return carry

    loads[1].wait()
    loads[2].wait()
    when_recv(4)
    grad_rows(1)
    taps(*OWN_ROW)
    acc[...] = grad_act(1, jnp.zeros(acc.shape, F32))

    for i in range(4):
        when_recv(i)
    grad_rows(0)
    grad_rows(2)
    for c in range(4):
        taps(*TAPS[c])
        hand_over(c)
    combine(0)
    down_terms()
    hand_over(DOWN)
    combine(1)
    acc[...] = grad_act(0, acc[...])
    relay(0)
    combine(2)
    acc[...] = grad_act(2, acc[...])
    relay(1)
    combine(3)
    turn(0)
    lax.fori_loop(0, 4, finish, 0)
    store = pltpu.make_async_copy(held, g_in, loc_sem.at[0])
    store.start()
    combine(DOWN)
    relay(2)
    turn(1)
    leave(0)
    relay(3)
    turn(2)
    leave(1)
    relay(DOWN)
    turn(3)
    leave(2)
    turn(DOWN)
    leave(3)
    leave(DOWN)

    mine = lax.rem(z, 2)
    for s in range(8):
        @pl.when(jnp.logical_not((z == s) & (core == mine)))
        def _():
            remote(ztd.at[0], zrd.at[s], zsd.at[0, 0], zrds.at[s], partner).wait_recv()
            remote(zt.at[0, 0], zr.at[s], zs.at[0, 0], zrs.at[s], partner).wait_recv()

    x_odd = lax.rem(x, 2) == 1
    total = zr[0].astype(F32)
    total_d = zrd[0].astype(F32)
    for s in range(1, 8):
        total = total + zr[s].astype(F32)
        total_d = total_d + zrd[s].astype(F32)
    whole = jnp.concatenate([total, pltpu.roll(total, 64, 1)[16:64]], axis=0)
    whole = jnp.where(x_odd, pltpu.roll(whole, 108, 0), whole)
    sums[0:112] = whole
    total_d = jnp.where(core == 1, pltpu.roll(total_d, 64, 1), total_d)
    total_d = jnp.where(x_odd, pltpu.roll(total_d, 12, 0), total_d)
    sums[112:128] = total_d
    store.wait()

    for i in range(6):
        @pl.when(halo[i][3])
        def _():
            copies[i].wait_send()

    for c in range(5):
        for i in range(10):
            message(c, i).wait_send()
    for c in range(4):
        for k in range(2):
            z_wait(zt.at[c, k], zr, zs.at[c, k], zrs, 2 * c + core, k)
            z_wait(ztd.at[c], zrd, zsd.at[c, k], zrds, 2 * c + core, k)


def hand_out(given, sums, g_in, g_conv, g_down):
    g_in[...] = given[...]
    g_conv[...] = sums[0:112].T[0:64, 0:108]
    g_down[...] = sums[112:124, 0:64]


def body(clip, weight, down, gout):
    vmem = pltpu.VMEM
    chunk = []
    for n in SIZES:
        full, pair = (4, 4, n, 128), (2, 2, n, 128)
        chunk += [vmem(s, BF16) for s in (full, full, full, pair, pair, pair, pair)]
        later = BF16 if n == 112 else F32
        chunk += [vmem((4, n, 128), later), vmem((3, n, 128), later)]
    dma = pltpu.SemaphoreType.DMA
    scratch = [
        vmem((3, 3, 3, CH, CH), BF16),
        vmem((3, CH, CH), BF16),
        vmem((6, COLS, CH), BF16),
        vmem((3, 4, COLS, CH), BF16),
        vmem((3, 6, COLS, CH), BF16),
        vmem((CH, 4 * COLS), BF16),
        vmem((3, 3, 6, COLS, CH), BF16),
        vmem((3, 4, COLS, CH), BF16),
        vmem((4 * COLS, CH), F32),
        vmem((27 * CH, CH), F32),
        vmem((3 * CH, CH), F32),
        vmem((4, 1, COLS, CH), BF16),
        vmem((4, 2, 64, 128), BF16),
        vmem((4, 16, 128), F32),
        vmem((8, 64, 128), BF16),
        vmem((8, 16, 128), F32),
        *chunk,
        dma((6,)),
        dma((6,)),
        dma((6,)),
        dma((5, 10)),
        dma((5, 10)),
        dma((4, 2)),
        dma((4, 2)),
        dma((8,)),
        dma((8,)),
    ]
    g_in, sums = pl.pallas_call(
        kernel,
        out_shape=(jax.ShapeDtypeStruct(clip.shape, BF16), jax.ShapeDtypeStruct((128, 128), F32)),
        in_specs=[pl.BlockSpec(memory_space=pl.ANY)] * 4,
        out_specs=[pl.BlockSpec(memory_space=pl.ANY), pl.BlockSpec(memory_space=vmem)],
        scratch_shapes=scratch,
        compiler_params=pltpu.CompilerParams(collective_id=0, has_side_effects=True),
        name="block_backward",
    )(clip, weight, down, gout)
    g_in, g_conv, g_down = pl.pallas_call(
        hand_out,
        out_shape=(
            jax.ShapeDtypeStruct(clip.shape, BF16),
            jax.ShapeDtypeStruct((64, 108), F32),
            jax.ShapeDtypeStruct((12, 64), F32),
        ),
        in_specs=[pl.BlockSpec(memory_space=vmem)] * 2,
        out_specs=[pl.BlockSpec(memory_space=vmem)] * 3,
        name="hand_out",
    )(g_in, sums)
    return g_in, g_conv.T, g_down


def solution(mesh):
    placed = (P("tm", "height", None, None), P(), P(), P("tm", "height", None, None))
    return jax.shard_map(
        body,
        mesh=mesh,
        in_specs=placed,
        out_specs=(P("tm", "height", None, None), P("height", "tm"), P("height", "tm")),
        check_vma=False,
    )
```

```python
import jax
import jax.numpy as jnp
from jax import lax
from jax.experimental import pallas as pl
from jax.experimental.pallas import tpu as pltpu
from jax.sharding import PartitionSpec as P

MESH = pl.DeviceIdType.MESH
F32 = jnp.float32
BF16 = jnp.bfloat16
COLS = 128
CH = 256
SIZES = (112, 112, 112, 112, 64)
DOWN = 4
OWN_ROW = (1, 3, 3)
TAPS = ((0, 5, 2), (2, 4, 2), (3, 0, 1), (8, 0, 1))


def nt(lhs, rhs):
    return lax.dot_general(lhs, rhs, (((1,), (1,)), ((), ())), preferred_element_type=F32)


def nn(lhs, rhs):
    return jnp.dot(lhs, rhs, preferred_element_type=F32)


def sigmoid(value):
    return 1.0 / (1.0 + jnp.exp(-value))


def shifted(value, row):
    before = jnp.where(row == 0, 0.0, pltpu.roll(value, 1, 0))
    after = jnp.where(row == COLS - 1, 0.0, pltpu.roll(value, COLS - 1, 0))
    return before, after


def kernel(clip, weight, down, gout, g_in, sums, *scratch):
    scratch = list(scratch)
    take = lambda n: [scratch.pop(0) for _ in range(n)]
    (wgt, dwn, cl, go, acts, act_t, gs, cb, acc, part, part_d, held) = take(12)
    (zt, ztd, zr, zrd) = take(4)
    bufs = [take(9) for _ in SIZES]
    (loc_sem, halo_s, halo_r, red_s, red_r, zs, zsd, zrs, zrds) = take(9)

    tm = lax.axis_index("tm")
    h = lax.axis_index("height")
    core = lax.rem(tm, 2)
    yh = lax.div(tm, 2)
    x = lax.rem(h, 4)
    z = lax.rem(lax.div(h, 4), 8)
    yl = lax.div(h, 32)
    y = yh * 2 + yl

    def dev(xx, yy, zz, cc):
        return (lax.div(yy, 2) * 2 + cc, lax.rem(yy, 2) * 32 + zz * 4 + xx)

    def near(dt, dh):
        return (lax.rem(tm + dt + 4, 4), lax.rem(h + dh + 64, 64))

    def first(d):
        return dev(lax.rem(x + (1 - core) * d, 4), lax.rem(y + core * d, 4), z, core)

    def second(d):
        return dev(lax.rem(x + core * d, 4), lax.rem(y + (1 - core) * d, 4), z, core)

    def remote(src, dst, send, recv, device):
        return pltpu.make_async_remote_copy(
            src_ref=src, dst_ref=dst, send_sem=send, recv_sem=recv, device_id=device, device_id_type=MESH
        )

    barrier = pltpu.get_barrier_semaphore()
    peers = [near(dt, dh) for dt in (-1, 1) for dh in (-1, 0, 1)] + [near(0, -1), near(0, 1)]
    peers += [first(d) for d in (1, 2, 3)] + [second(d) for d in (1, 2, 3)]
    peers += [dev(x, y, lax.rem(z + d, 8), c) for d in range(1, 8) for c in (0, 1)]
    for peer in peers:
        pl.semaphore_signal(barrier, inc=1, device_id=peer, device_id_type=MESH)

    loads = [
        pltpu.make_async_copy(clip.at[:, 0], cl.at[pl.ds(2, 4)], loc_sem.at[0]),
        pltpu.make_async_copy(gout.at[:, 0], go.at[1, pl.ds(0, 2)], loc_sem.at[1]),
        pltpu.make_async_copy(down, dwn, loc_sem.at[2]),
    ] + [pltpu.make_async_copy(weight.at[a], wgt.at[a], loc_sem.at[3 + a]) for a in range(3)]
    for load in loads:
        load.start()

    pl.semaphore_wait(barrier, len(peers))

    halo = [
        (gout.at[:, 0], go.at[0, pl.ds(0, 2)], near(0, 1), h < 63, h > 0),
        (gout.at[:, 0], go.at[2, pl.ds(0, 2)], near(0, -1), h > 0, h < 63),
        (clip.at[pl.ds(2, 2), 0], cl.at[pl.ds(0, 2)], near(1, 0), tm < 3, tm > 0),
    ]
    for frame in range(2):
        late = gout.at[pl.ds(frame, 1), 0]
        place = pl.ds(2 + frame, 1)
        halo += [
            (late, go.at[1, place], near(-1, 0), tm > 0, tm < 3),
            (late, go.at[0, place], near(-1, 1), (tm > 0) & (h < 63), (tm < 3) & (h > 0)),
            (late, go.at[2, place], near(-1, -1), (tm > 0) & (h > 0), (tm < 3) & (h < 63)),
        ]
    copies = [remote(s, d, halo_s.at[i], halo_r.at[i], to) for i, (s, d, to, _, _) in enumerate(halo)]

    def when_start(i):
        @pl.when(halo[i][3])
        def _():
            copies[i].start()

    def when_recv(i):
        @pl.when(halo[i][4])
        def _():
            copies[i].wait_recv()

        @pl.when(jnp.logical_not(halo[i][4]))
        def _():
            dst = halo[i][1]
            dst[...] = jnp.zeros(dst.shape, BF16)

    for i in (3, 2, 4, 5, 0, 1, 6, 7, 8):
        when_start(i)

    row = lax.broadcasted_iota(jnp.int32, (COLS, CH), 0)

    def act_frame(f, carry):
        value = cl[f].astype(F32)
        act = value * sigmoid(value)
        before, after = shifted(act, row)
        acts[0, f] = before.astype(BF16)
        acts[1, f] = act.astype(BF16)
        acts[2, f] = after.astype(BF16)
        act_t[f] = act.T.astype(BF16)
        return carry

    loads[0].wait()
    lax.fori_loop(2, 6, act_frame, 0)
    def conv_rows(b, carry):
        total = jnp.zeros((4 * COLS, CH), F32)
        for a in range(3):
            lhs = jnp.concatenate([acts[c, pl.ds(a, 4)].reshape(4 * COLS, CH) for c in range(3)], axis=1)
            total = total + nn(lhs, wgt[a, b].reshape(3 * CH, CH))
        own = cl[pl.ds(2, 4)].reshape(4 * COLS, CH).astype(F32)
        total = total + jnp.where(b == 1, own, 0.0)
        cb[b] = total.astype(BF16).reshape(4, COLS, CH)
        return carry

    def grad_rows(r):
        later = go[r, pl.ds(1, 2)].reshape(2 * COLS, CH)
        here = go[r, pl.ds(0, 2)].reshape(2 * COLS, CH)
        even = nt(later, dwn[0]) + nt(here, dwn[2])
        odd = nt(later, dwn[1])
        for v in range(2):
            place(r, 2 * v, even[v * COLS : (v + 1) * COLS])
            place(r, 2 * v + 1, odd[v * COLS : (v + 1) * COLS])

    def place(r, f, value):
        before, after = shifted(value, row)
        gs[0, r, f] = after.astype(BF16)
        gs[1, r, f] = value.astype(BF16)
        gs[2, r, f] = before.astype(BF16)

    def grad_tail():
        later = jnp.concatenate([go[r, 3] for r in range(3)], axis=0)
        here = jnp.concatenate([go[r, 2] for r in range(3)], axis=0)
        even = nt(later, dwn[0]) + nt(here, dwn[2])
        odd = nt(later, dwn[1])
        for r in range(3):
            place(r, 4, even[r * COLS : (r + 1) * COLS])
            place(r, 5, odd[r * COLS : (r + 1) * COLS])

    def down_terms():
        for k, pairs in ((0, ((0, 1), (2, 2))), (1, ((1, 1), (3, 2))), (2, ((0, 0), (2, 1)))):
            lhs = jnp.concatenate([cb[b, t] for b in range(3) for t, _ in pairs], axis=0)
            rhs = jnp.concatenate([go[2 - b, u] for b in range(3) for _, u in pairs], axis=0)
            part_d[k * CH : (k + 1) * CH, :] = lax.dot_general(
                lhs, rhs, (((0,), (0,)), ((), ())), preferred_element_type=F32
            )

    def taps(start, step, count):
        def one(i, carry):
            ab = start + step * i
            a, b = lax.div(ab, 3), lax.rem(ab, 3)
            lhs = jnp.concatenate([act_t[a + f] for f in range(4)], axis=1)
            for s in range(3):
                rhs = gs[s, 2 - b, pl.ds(0, 4)].reshape(4 * COLS, CH)
                part[pl.ds(pl.multiple_of((3 * ab + s) * CH, CH), CH), :] = nn(lhs, rhs)
            return carry

        lax.fori_loop(0, count, one, 0)

    def blocks(c, cc, put):
        def two(i, carry):
            l, pair = lax.div(i, 2), lax.rem(i, 2)
            if c == DOWN:
                for j in range(4):
                    base = pl.multiple_of(24 * (16 * l + 2 * (2 * j + cc) + pair), 8)
                    each(part_d, base, 16, 8, slice(16 * j, 16 * j + 16), l, pair)
            else:
                base = pl.multiple_of(216 * (16 * l + 2 * (2 * c + cc) + pair), 8)
                each(part, base, 112, 104, slice(0, 112), l, pair)
            return carry

        def each(src, base, size, skip, where, l, pair):
            for odd in range(2):
                value = src[pl.ds(base + skip * odd, size), :]
                xx = 2 * pair + odd
                for hi in range(2):
                    yy = 2 * hi + l
                    p = (1 - cc) * xx + cc * yy
                    q = (1 - cc) * yy + cc * xx
                    put(p, q, where, value[:, 128 * hi : 128 * hi + 128])

        lax.fori_loop(0, 4, two, 0)

    partner = dev(x, y, z, 1 - core)
    p0 = (1 - core) * x + core * y
    q0 = (1 - core) * y + core * x
    pn, pp, po = lax.rem(p0 + 1, 4), lax.rem(p0 + 3, 4), lax.rem(p0 + 2, 4)

    def message(c, i):
        s_, sr, b_, leg, dr, cs, cm, r_, rx = bufs[c]
        lo, hi = pl.ds(0, 2), pl.ds(2, 2)
        if i == 0:
            src, dst, to = s_, sr, partner
        elif i == 1:
            src, dst, to = b_.at[po, lo], leg.at[0], first(1)
        elif i == 2:
            src, dst, to = b_.at[po, hi], leg.at[1], first(3)
        elif i == 3:
            src, dst, to = b_.at[pn, hi], dr.at[0], first(1)
        elif i == 4:
            src, dst, to = b_.at[pp, lo], dr.at[1], first(3)
        elif i == 5:
            src, dst, to = cs.at[0], cm.at[0], first(1)
        elif i == 6:
            src, dst, to = cs.at[1], cm.at[1], first(3)
        else:
            d = i - 6
            src, dst, to = r_.at[lax.rem(q0 + d, 4)], rx.at[d - 1], second(d)
        return remote(src, dst, red_s.at[c, i], red_r.at[c, i], to)

    def hand_over(c):
        s_ = bufs[c][0]

        def put(p, q, where, value):
            s_[p, q, where] = value.astype(BF16)

        blocks(c, 1 - core, put)
        message(c, 0).start()

    def combine(c):
        sr, b_ = bufs[c][1], bufs[c][2]
        message(c, 0).wait_recv()

        def put(p, q, where, value):
            b_[p, q, where] = (value + sr[p, q, where].astype(F32)).astype(BF16)

        blocks(c, core, put)
        for i in (1, 2, 3, 4):
            message(c, i).start()

    def relay(c):
        _, _, b_, leg, _, cs, _, _, _ = bufs[c]
        message(c, 1).wait_recv()
        cs[0] = (b_[pn, pl.ds(0, 2)].astype(F32) + leg[0].astype(F32)).astype(BF16)
        message(c, 5).start()
        message(c, 2).wait_recv()
        cs[1] = (b_[pp, pl.ds(2, 2)].astype(F32) + leg[1].astype(F32)).astype(BF16)
        message(c, 6).start()

    def turn(c):
        _, _, b_, _, dr, _, cm, r_, _ = bufs[c]
        for i in (3, 4, 5, 6):
            message(c, i).wait_recv()
        for half in range(2):
            both = pl.ds(2 * half, 2)
            total = b_[p0, both].astype(F32) + cm[half].astype(F32) + dr[1 - half].astype(F32)
            r_[both] = total.astype(r_.dtype)
        for i in (7, 8, 9):
            message(c, i).start()

    lane = lax.broadcasted_iota(jnp.int32, (64, 128), 1)

    def z_send(src, dst, keep, send, recv, to_z, k):
        own = (to_z == z) & (core == k)

        @pl.when(own)
        def _():
            dst.at[z][...] = src[...]

        @pl.when(jnp.logical_not(own))
        def _():
            remote(src, dst.at[z], send, recv.at[z], dev(x, y, to_z, k)).start()

    def z_wait(src, dst, send, recv, to_z, k):
        @pl.when(jnp.logical_not((to_z == z) & (core == k)))
        def _():
            remote(src, dst.at[z], send, recv.at[z], dev(x, y, to_z, k)).wait_send()

    def leave(c):
        r_, rx = bufs[c][7], bufs[c][8]
        for i in (7, 8, 9):
            message(c, i).wait_recv()
        total = r_[q0].astype(F32)
        for d in range(3):
            total = total + rx[d].astype(F32)
        if c == DOWN:
            ztd[...] = total.reshape(4, 16, 128)
            for j in range(4):
                for k in range(2):
                    z_send(ztd.at[j], zrd, None, zsd.at[j, k], zrds, 2 * j + core, k)
        else:
            top, low = total[0:64], total[48:112]
            zt[c, 0] = jnp.where(lane < 64, top, pltpu.roll(low, 64, 1)).astype(BF16)
            zt[c, 1] = jnp.where(lane < 64, pltpu.roll(top, 64, 1), low).astype(BF16)
            for k in range(2):
                z_send(zt.at[c, k], zr, None, zs.at[c, k], zrs, 2 * c + core, k)

    def grad_act(b, total):
        for a in range(3):
            for s in range(3):
                total = total + nt(gs[s, 2 - b, pl.ds(2 - a, 4)].reshape(4 * COLS, CH), wgt[a, b, s])
        return total

    def finish(f, carry):
        value = cl[f + 2].astype(F32)
        sig = sigmoid(value)
        grad = acc[pl.ds(pl.multiple_of(f * COLS, COLS), COLS), :]
        held[f, 0] = (gs[1, 1, f].astype(F32) + grad * (sig * (1.0 + value * (1.0 - sig)))).astype(BF16)
        return carry

    loads[1].wait()
    loads[2].wait()
    when_recv(3)
    grad_rows(1)
    when_recv(2)
    lax.fori_loop(0, 2, act_frame, 0)
    taps(*OWN_ROW)
    for a in range(3):
        loads[3 + a].wait()
    for i in (0, 1, 4, 5):
        when_recv(i)
    grad_rows(0)
    grad_rows(2)
    for c in range(4):
        taps(*TAPS[c])
        hand_over(c)
    combine(0)
    combine(1)
    combine(2)
    combine(3)
    lax.fori_loop(0, 3, conv_rows, 0)
    relay(0)
    when_recv(6)
    when_recv(7)
    when_recv(8)
    down_terms()
    hand_over(DOWN)
    grad_tail()
    relay(1)
    combine(DOWN)
    relay(2)
    acc[...] = grad_act(0, jnp.zeros(acc.shape, F32))
    relay(3)
    turn(0)
    acc[...] = grad_act(1, acc[...])
    relay(DOWN)
    turn(1)
    acc[...] = grad_act(2, acc[...])
    turn(2)
    leave(0)
    lax.fori_loop(0, 4, finish, 0)
    store = pltpu.make_async_copy(held, g_in, loc_sem.at[0])
    store.start()
    turn(3)
    leave(1)
    turn(DOWN)
    leave(2)
    leave(3)
    leave(DOWN)

    mine = lax.rem(z, 2)
    for s in range(8):
        @pl.when(jnp.logical_not((z == s) & (core == mine)))
        def _():
            remote(ztd.at[0], zrd.at[s], zsd.at[0, 0], zrds.at[s], partner).wait_recv()
            remote(zt.at[0, 0], zr.at[s], zs.at[0, 0], zrs.at[s], partner).wait_recv()

    x_odd = lax.rem(x, 2) == 1
    total = zr[0].astype(F32)
    total_d = zrd[0].astype(F32)
    for s in range(1, 8):
        total = total + zr[s].astype(F32)
        total_d = total_d + zrd[s].astype(F32)
    whole = jnp.concatenate([total, pltpu.roll(total, 64, 1)[16:64]], axis=0)
    whole = jnp.where(x_odd, pltpu.roll(whole, 108, 0), whole)
    sums[0:112] = whole
    total_d = jnp.where(core == 1, pltpu.roll(total_d, 64, 1), total_d)
    total_d = jnp.where(x_odd, pltpu.roll(total_d, 12, 0), total_d)
    sums[112:128] = total_d
    store.wait()

    for i in range(9):
        @pl.when(halo[i][3])
        def _():
            copies[i].wait_send()

    for c in range(5):
        for i in range(10):
            message(c, i).wait_send()
    for c in range(4):
        for k in range(2):
            z_wait(zt.at[c, k], zr, zs.at[c, k], zrs, 2 * c + core, k)
            z_wait(ztd.at[c], zrd, zsd.at[c, k], zrds, 2 * c + core, k)


def hand_out(given, sums, g_in, g_conv, g_down):
    g_in[...] = given[...]
    g_conv[...] = sums[0:112].T[0:64, 0:108]
    g_down[...] = sums[112:124, 0:64]


def body(clip, weight, down, gout):
    vmem = pltpu.VMEM
    chunk = []
    for n in SIZES:
        full, pair = (4, 4, n, 128), (2, 2, n, 128)
        chunk += [vmem(s, BF16) for s in (full, full, full, pair, pair, pair, pair)]
        later = BF16 if n == 112 else F32
        chunk += [vmem((4, n, 128), later), vmem((3, n, 128), later)]
    dma = pltpu.SemaphoreType.DMA
    scratch = [
        vmem((3, 3, 3, CH, CH), BF16),
        vmem((3, CH, CH), BF16),
        vmem((6, COLS, CH), BF16),
        vmem((3, 4, COLS, CH), BF16),
        vmem((3, 6, COLS, CH), BF16),
        vmem((6, CH, COLS), BF16),
        vmem((3, 3, 6, COLS, CH), BF16),
        vmem((3, 4, COLS, CH), BF16),
        vmem((4 * COLS, CH), F32),
        vmem((27 * CH, CH), F32),
        vmem((3 * CH, CH), F32),
        vmem((4, 1, COLS, CH), BF16),
        vmem((4, 2, 64, 128), BF16),
        vmem((4, 16, 128), F32),
        vmem((8, 64, 128), BF16),
        vmem((8, 16, 128), F32),
        *chunk,
        dma((6,)),
        dma((9,)),
        dma((9,)),
        dma((5, 10)),
        dma((5, 10)),
        dma((4, 2)),
        dma((4, 2)),
        dma((8,)),
        dma((8,)),
    ]
    g_in, sums = pl.pallas_call(
        kernel,
        out_shape=(jax.ShapeDtypeStruct(clip.shape, BF16), jax.ShapeDtypeStruct((128, 128), F32)),
        in_specs=[pl.BlockSpec(memory_space=pl.ANY)] * 4,
        out_specs=[pl.BlockSpec(memory_space=pl.ANY), pl.BlockSpec(memory_space=vmem)],
        scratch_shapes=scratch,
        compiler_params=pltpu.CompilerParams(collective_id=0, has_side_effects=True),
        name="block_backward",
    )(clip, weight, down, gout)
    g_in, g_conv, g_down = pl.pallas_call(
        hand_out,
        out_shape=(
            jax.ShapeDtypeStruct(clip.shape, BF16),
            jax.ShapeDtypeStruct((64, 108), F32),
            jax.ShapeDtypeStruct((12, 64), F32),
        ),
        in_specs=[pl.BlockSpec(memory_space=vmem)] * 2,
        out_specs=[pl.BlockSpec(memory_space=vmem)] * 3,
        name="hand_out",
    )(g_in, sums)
    return g_in, g_conv.T, g_down


def solution(mesh):
    placed = (P("tm", "height", None, None), P(), P(), P("tm", "height", None, None))
    return jax.shard_map(
        body,
        mesh=mesh,
        in_specs=placed,
        out_specs=(P("tm", "height", None, None), P("height", "tm"), P("height", "tm")),
        check_vma=False,
    )
```

```python
import jax
import jax.numpy as jnp
from jax import lax
from jax.experimental import pallas as pl
from jax.experimental.pallas import tpu as pltpu
from jax.sharding import PartitionSpec as P

MESH = pl.DeviceIdType.MESH
F32 = jnp.float32
BF16 = jnp.bfloat16
COLS = 128
CH = 256
SIZES = (112, 112, 112, 112, 64)
DOWN = 4
OWN_ROW = (1, 3, 3)
TAPS = ((0, 5, 2), (2, 4, 2), (3, 0, 1), (8, 0, 1))


def nt(lhs, rhs):
    return lax.dot_general(lhs, rhs, (((1,), (1,)), ((), ())), preferred_element_type=F32)


def nn(lhs, rhs):
    return jnp.dot(lhs, rhs, preferred_element_type=F32)


def sigmoid(value):
    return 1.0 / (1.0 + jnp.exp(-value))


def shifted(value, row):
    before = jnp.where(row == 0, 0.0, pltpu.roll(value, 1, 0))
    after = jnp.where(row == COLS - 1, 0.0, pltpu.roll(value, COLS - 1, 0))
    return before, after


def kernel(clip, weight, down, gout, g_in, sums, *scratch):
    scratch = list(scratch)
    take = lambda n: [scratch.pop(0) for _ in range(n)]
    (wgt, dwn, cl, go, acts, act_t, gs, cb, acc, part, part_d, held) = take(12)
    (zt, ztd, zr, zrd) = take(4)
    bufs = [take(9) for _ in SIZES]
    (loc_sem, halo_s, halo_r, red_s, red_r, zs, zsd, zrs, zrds, up, low) = take(11)

    tm = lax.axis_index("tm")
    h = lax.axis_index("height")
    core = lax.rem(tm, 2)
    yh = lax.div(tm, 2)
    x = lax.rem(h, 4)
    z = lax.rem(lax.div(h, 4), 8)
    yl = lax.div(h, 32)
    y = yh * 2 + yl

    def dev(xx, yy, zz, cc):
        return (lax.div(yy, 2) * 2 + cc, lax.rem(yy, 2) * 32 + zz * 4 + xx)

    def near(dt, dh):
        return (lax.rem(tm + dt + 4, 4), lax.rem(h + dh + 64, 64))

    def first(d):
        return dev(lax.rem(x + (1 - core) * d, 4), lax.rem(y + core * d, 4), z, core)

    def second(d):
        return dev(lax.rem(x + core * d, 4), lax.rem(y + (1 - core) * d, 4), z, core)

    def remote(src, dst, send, recv, device):
        return pltpu.make_async_remote_copy(
            src_ref=src, dst_ref=dst, send_sem=send, recv_sem=recv, device_id=device, device_id_type=MESH
        )

    barrier = pltpu.get_barrier_semaphore()
    ring = [first(d) for d in (1, 2, 3)] + [second(d) for d in (1, 2, 3)]
    ring += [dev(x, y, lax.rem(z + d, 8), core) for d in (1, 7)]
    for peer in ring:
        pl.semaphore_signal(barrier, inc=1, device_id=peer, device_id_type=MESH)
    has_h = {-1: lax.div(h + 62, 63), 0: 1, 1: lax.div(125 - h, 63)}
    has_t = {-1: lax.div(tm + 2, 3), 0: 1, 1: lax.div(5 - tm, 3)}
    expected = len(ring)
    for dt, dh in ((-1, 0), (1, 0), (0, -1), (0, 1), (-1, -1), (-1, 1), (1, -1), (1, 1)):
        there = has_t[dt] * has_h[dh]
        expected = expected + there

        @pl.when(there == 1)
        def _():
            pl.semaphore_signal(barrier, inc=1, device_id=near(dt, dh), device_id_type=MESH)

    loads = [
        pltpu.make_async_copy(clip.at[:, 0], cl.at[pl.ds(2, 4)], loc_sem.at[0]),
        pltpu.make_async_copy(gout.at[:, 0], go.at[1, pl.ds(0, 2)], loc_sem.at[1]),
        pltpu.make_async_copy(down, dwn, loc_sem.at[2]),
    ] + [pltpu.make_async_copy(weight.at[a], wgt.at[a], loc_sem.at[3 + a]) for a in range(3)]
    for load in loads:
        load.start()

    pl.semaphore_wait(barrier, expected)

    above, below = dev(x, y, lax.rem(z + 1, 8), core), dev(x, y, lax.rem(z + 7, 8), core)

    def tell(level):
        pl.semaphore_signal(up.at[level], inc=1, device_id=below, device_id_type=MESH)
        if level < 3:
            pl.semaphore_signal(low.at[level], inc=1, device_id=above, device_id_type=MESH)

    def hear(level):
        pl.semaphore_wait(up.at[level], 1)
        if level < 3:
            pl.semaphore_wait(low.at[level], 1)

    tell(0)

    halo = [
        (gout.at[:, 0], go.at[0, pl.ds(0, 2)], near(0, 1), h < 63, h > 0),
        (gout.at[:, 0], go.at[2, pl.ds(0, 2)], near(0, -1), h > 0, h < 63),
        (clip.at[pl.ds(2, 2), 0], cl.at[pl.ds(0, 2)], near(1, 0), tm < 3, tm > 0),
    ]
    for frame in range(2):
        late = gout.at[pl.ds(frame, 1), 0]
        place = pl.ds(2 + frame, 1)
        halo += [
            (late, go.at[1, place], near(-1, 0), tm > 0, tm < 3),
            (late, go.at[0, place], near(-1, 1), (tm > 0) & (h < 63), (tm < 3) & (h > 0)),
            (late, go.at[2, place], near(-1, -1), (tm > 0) & (h > 0), (tm < 3) & (h < 63)),
        ]
    copies = [remote(s, d, halo_s.at[i], halo_r.at[i], to) for i, (s, d, to, _, _) in enumerate(halo)]

    def when_start(i):
        @pl.when(halo[i][3])
        def _():
            copies[i].start()

    def when_recv(i):
        @pl.when(halo[i][4])
        def _():
            copies[i].wait_recv()

        @pl.when(jnp.logical_not(halo[i][4]))
        def _():
            dst = halo[i][1]
            dst[...] = jnp.zeros(dst.shape, BF16)

    for i in (3, 2, 4, 5, 0, 1):
        when_start(i)

    row = lax.broadcasted_iota(jnp.int32, (COLS, CH), 0)

    def act_frame(f, carry):
        value = cl[f].astype(F32)
        act = value * sigmoid(value)
        before, after = shifted(act, row)
        acts[0, f] = before.astype(BF16)
        acts[1, f] = act.astype(BF16)
        acts[2, f] = after.astype(BF16)
        act_t[f] = act.T.astype(BF16)
        return carry

    loads[0].wait()
    lax.fori_loop(2, 6, act_frame, 0)
    def conv_rows(b, carry):
        total = jnp.zeros((4 * COLS, CH), F32)
        for a in range(3):
            lhs = jnp.concatenate([acts[c, pl.ds(a, 4)].reshape(4 * COLS, CH) for c in range(3)], axis=1)
            total = total + nn(lhs, wgt[a, b].reshape(3 * CH, CH))
        own = cl[pl.ds(2, 4)].reshape(4 * COLS, CH).astype(F32)
        total = total + jnp.where(b == 1, own, 0.0)
        cb[b] = total.astype(BF16).reshape(4, COLS, CH)
        return carry

    def grad_rows(r):
        later = go[r, pl.ds(1, 2)].reshape(2 * COLS, CH)
        here = go[r, pl.ds(0, 2)].reshape(2 * COLS, CH)
        even = nt(later, dwn[0]) + nt(here, dwn[2])
        odd = nt(later, dwn[1])
        for v in range(2):
            place(r, 2 * v, even[v * COLS : (v + 1) * COLS])
            place(r, 2 * v + 1, odd[v * COLS : (v + 1) * COLS])

    def place(r, f, value):
        before, after = shifted(value, row)
        gs[0, r, f] = after.astype(BF16)
        gs[1, r, f] = value.astype(BF16)
        gs[2, r, f] = before.astype(BF16)

    def grad_tail():
        later = jnp.concatenate([go[r, 3] for r in range(3)], axis=0)
        here = jnp.concatenate([go[r, 2] for r in range(3)], axis=0)
        even = nt(later, dwn[0]) + nt(here, dwn[2])
        odd = nt(later, dwn[1])
        for r in range(3):
            place(r, 4, even[r * COLS : (r + 1) * COLS])
            place(r, 5, odd[r * COLS : (r + 1) * COLS])

    def down_terms():
        for k, pairs in ((0, ((0, 1), (2, 2))), (1, ((1, 1), (3, 2))), (2, ((0, 0), (2, 1)))):
            lhs = jnp.concatenate([cb[b, t] for b in range(3) for t, _ in pairs], axis=0)
            rhs = jnp.concatenate([go[2 - b, u] for b in range(3) for _, u in pairs], axis=0)
            part_d[k * CH : (k + 1) * CH, :] = lax.dot_general(
                lhs, rhs, (((0,), (0,)), ((), ())), preferred_element_type=F32
            )

    def taps(start, step, count):
        def one(i, carry):
            ab = start + step * i
            a, b = lax.div(ab, 3), lax.rem(ab, 3)
            lhs = jnp.concatenate([act_t[a + f] for f in range(4)], axis=1)
            for s in range(3):
                rhs = gs[s, 2 - b, pl.ds(0, 4)].reshape(4 * COLS, CH)
                part[pl.ds(pl.multiple_of((3 * ab + s) * CH, CH), CH), :] = nn(lhs, rhs)
            return carry

        lax.fori_loop(0, count, one, 0)

    def blocks(c, cc, put):
        def two(i, carry):
            l, pair = lax.div(i, 2), lax.rem(i, 2)
            if c == DOWN:
                for j in range(4):
                    base = pl.multiple_of(24 * (16 * l + 2 * (2 * j + cc) + pair), 8)
                    each(part_d, base, 16, 8, slice(16 * j, 16 * j + 16), l, pair)
            else:
                base = pl.multiple_of(216 * (16 * l + 2 * (2 * c + cc) + pair), 8)
                each(part, base, 112, 104, slice(0, 112), l, pair)
            return carry

        def each(src, base, size, skip, where, l, pair):
            for odd in range(2):
                value = src[pl.ds(base + skip * odd, size), :]
                xx = 2 * pair + odd
                for hi in range(2):
                    yy = 2 * hi + l
                    p = (1 - cc) * xx + cc * yy
                    q = (1 - cc) * yy + cc * xx
                    put(p, q, where, value[:, 128 * hi : 128 * hi + 128])

        lax.fori_loop(0, 4, two, 0)

    partner = dev(x, y, z, 1 - core)
    p0 = (1 - core) * x + core * y
    q0 = (1 - core) * y + core * x
    pn, pp, po = lax.rem(p0 + 1, 4), lax.rem(p0 + 3, 4), lax.rem(p0 + 2, 4)

    def message(c, i):
        s_, sr, b_, leg, dr, cs, cm, r_, rx = bufs[c]
        lo, hi = pl.ds(0, 2), pl.ds(2, 2)
        if i == 0:
            src, dst, to = s_, sr, partner
        elif i == 1:
            src, dst, to = b_.at[po, lo], leg.at[0], first(1)
        elif i == 2:
            src, dst, to = b_.at[po, hi], leg.at[1], first(3)
        elif i == 3:
            src, dst, to = b_.at[pn, hi], dr.at[0], first(1)
        elif i == 4:
            src, dst, to = b_.at[pp, lo], dr.at[1], first(3)
        elif i == 5:
            src, dst, to = cs.at[0], cm.at[0], first(1)
        elif i == 6:
            src, dst, to = cs.at[1], cm.at[1], first(3)
        else:
            d = i - 6
            src, dst, to = r_.at[lax.rem(q0 + d, 4)], rx.at[d - 1], second(d)
        return remote(src, dst, red_s.at[c, i], red_r.at[c, i], to)

    def hand_over(c):
        s_ = bufs[c][0]

        def put(p, q, where, value):
            s_[p, q, where] = value.astype(BF16)

        blocks(c, 1 - core, put)
        message(c, 0).start()

    def combine(c):
        sr, b_ = bufs[c][1], bufs[c][2]
        message(c, 0).wait_recv()

        def put(p, q, where, value):
            b_[p, q, where] = (value + sr[p, q, where].astype(F32)).astype(BF16)

        blocks(c, core, put)
        for i in (1, 2, 3, 4):
            message(c, i).start()

    def relay(c):
        _, _, b_, leg, _, cs, _, _, _ = bufs[c]
        message(c, 1).wait_recv()
        cs[0] = (b_[pn, pl.ds(0, 2)].astype(F32) + leg[0].astype(F32)).astype(BF16)
        message(c, 5).start()
        message(c, 2).wait_recv()
        cs[1] = (b_[pp, pl.ds(2, 2)].astype(F32) + leg[1].astype(F32)).astype(BF16)
        message(c, 6).start()

    def turn(c):
        _, _, b_, _, dr, _, cm, r_, _ = bufs[c]
        for i in (3, 4, 5, 6):
            message(c, i).wait_recv()
        for half in range(2):
            both = pl.ds(2 * half, 2)
            total = b_[p0, both].astype(F32) + cm[half].astype(F32) + dr[1 - half].astype(F32)
            r_[both] = total.astype(r_.dtype)
        for i in (7, 8, 9):
            message(c, i).start()

    lane = lax.broadcasted_iota(jnp.int32, (64, 128), 1)

    def z_send(src, dst, keep, send, recv, to_z, k):
        own = (to_z == z) & (core == k)

        @pl.when(own)
        def _():
            dst.at[z][...] = src[...]

        @pl.when(jnp.logical_not(own))
        def _():
            remote(src, dst.at[z], send, recv.at[z], dev(x, y, to_z, k)).start()

    def z_wait(src, dst, send, recv, to_z, k):
        @pl.when(jnp.logical_not((to_z == z) & (core == k)))
        def _():
            remote(src, dst.at[z], send, recv.at[z], dev(x, y, to_z, k)).wait_send()

    def leave(c):
        r_, rx = bufs[c][7], bufs[c][8]
        for i in (7, 8, 9):
            message(c, i).wait_recv()
        total = r_[q0].astype(F32)
        for d in range(3):
            total = total + rx[d].astype(F32)
        if c == DOWN:
            ztd[...] = total.reshape(4, 16, 128)
            for j in range(4):
                for k in range(2):
                    z_send(ztd.at[j], zrd, None, zsd.at[j, k], zrds, 2 * j + core, k)
        else:
            top, low = total[0:64], total[48:112]
            zt[c, 0] = jnp.where(lane < 64, top, pltpu.roll(low, 64, 1)).astype(BF16)
            zt[c, 1] = jnp.where(lane < 64, pltpu.roll(top, 64, 1), low).astype(BF16)
            for k in range(2):
                z_send(zt.at[c, k], zr, None, zs.at[c, k], zrs, 2 * c + core, k)

    def grad_act(b, total):
        for a in range(3):
            for s in range(3):
                total = total + nt(gs[s, 2 - b, pl.ds(2 - a, 4)].reshape(4 * COLS, CH), wgt[a, b, s])
        return total

    def finish(f, carry):
        value = cl[f + 2].astype(F32)
        sig = sigmoid(value)
        grad = acc[pl.ds(pl.multiple_of(f * COLS, COLS), COLS), :]
        held[f, 0] = (gs[1, 1, f].astype(F32) + grad * (sig * (1.0 + value * (1.0 - sig)))).astype(BF16)
        return carry

    for a in range(3):
        loads[3 + a].wait()

    def convolve():
        lax.fori_loop(0, 3, conv_rows, 0)

    def earlier():
        when_recv(2)
        lax.fori_loop(0, 2, act_frame, 0)

    @pl.when(tm != 2)
    def _():
        earlier()
        convolve()

    loads[1].wait()
    loads[2].wait()
    when_recv(3)
    grad_rows(1)

    @pl.when(tm == 2)
    def _():
        earlier()

    taps(*OWN_ROW)
    hear(0)
    tell(1)

    @pl.when(tm == 2)
    def _():
        convolve()

    for i in (0, 1, 4, 5):
        when_recv(i)
    for i in (6, 7, 8):
        when_start(i)
    grad_rows(0)
    grad_rows(2)
    taps(*TAPS[0])
    hand_over(0)
    taps(*TAPS[1])
    hand_over(1)
    combine(0)
    taps(*TAPS[2])
    hand_over(2)
    combine(1)
    taps(*TAPS[3])
    hand_over(3)
    down_terms()
    hand_over(DOWN)
    combine(2)
    combine(3)
    hear(1)
    tell(2)
    relay(0)
    combine(DOWN)
    relay(1)
    relay(2)
    relay(3)
    relay(DOWN)
    hear(2)
    tell(3)
    turn(0)
    turn(1)
    acc[...] = jnp.zeros(acc.shape, F32)
    for i in (6, 7, 8):
        when_recv(i)
    grad_tail()
    acc[...] = grad_act(0, acc[...])
    turn(2)
    turn(3)
    turn(DOWN)
    acc[...] = grad_act(1, acc[...])
    acc[...] = grad_act(2, acc[...])
    hear(3)
    leave(0)
    leave(1)
    leave(2)
    leave(3)
    leave(DOWN)
    lax.fori_loop(0, 4, finish, 0)
    store = pltpu.make_async_copy(held, g_in, loc_sem.at[0])
    store.start()

    mine = lax.rem(z, 2)
    for s in range(8):
        @pl.when(jnp.logical_not((z == s) & (core == mine)))
        def _():
            remote(ztd.at[0], zrd.at[s], zsd.at[0, 0], zrds.at[s], partner).wait_recv()
            remote(zt.at[0, 0], zr.at[s], zs.at[0, 0], zrs.at[s], partner).wait_recv()

    x_odd = lax.rem(x, 2) == 1
    total = zr[0].astype(F32)
    total_d = zrd[0].astype(F32)
    for s in range(1, 8):
        total = total + zr[s].astype(F32)
        total_d = total_d + zrd[s].astype(F32)
    whole = jnp.concatenate([total, pltpu.roll(total, 64, 1)[16:64]], axis=0)
    whole = jnp.where(x_odd, pltpu.roll(whole, 108, 0), whole)
    sums[0:112] = whole
    total_d = jnp.where(core == 1, pltpu.roll(total_d, 64, 1), total_d)
    total_d = jnp.where(x_odd, pltpu.roll(total_d, 12, 0), total_d)
    sums[112:128] = total_d
    store.wait()

    for i in range(9):
        @pl.when(halo[i][3])
        def _():
            copies[i].wait_send()

    for c in range(5):
        for i in range(10):
            message(c, i).wait_send()
    for c in range(4):
        for k in range(2):
            z_wait(zt.at[c, k], zr, zs.at[c, k], zrs, 2 * c + core, k)
            z_wait(ztd.at[c], zrd, zsd.at[c, k], zrds, 2 * c + core, k)


def hand_out(given, sums, g_in, g_conv, g_down):
    g_in[...] = given[...]
    g_conv[...] = sums[0:112].T[0:64, 0:108]
    g_down[...] = sums[112:124, 0:64]


def body(clip, weight, down, gout):
    vmem = pltpu.VMEM
    chunk = []
    for n in SIZES:
        full, pair = (4, 4, n, 128), (2, 2, n, 128)
        chunk += [vmem(s, BF16) for s in (full, full, full, pair, pair, pair, pair)]
        later = BF16 if n == 112 else F32
        chunk += [vmem((4, n, 128), later), vmem((3, n, 128), later)]
    dma = pltpu.SemaphoreType.DMA
    scratch = [
        vmem((3, 3, 3, CH, CH), BF16),
        vmem((3, CH, CH), BF16),
        vmem((6, COLS, CH), BF16),
        vmem((3, 4, COLS, CH), BF16),
        vmem((3, 6, COLS, CH), BF16),
        vmem((6, CH, COLS), BF16),
        vmem((3, 3, 6, COLS, CH), BF16),
        vmem((3, 4, COLS, CH), BF16),
        vmem((4 * COLS, CH), F32),
        vmem((27 * CH, CH), F32),
        vmem((3 * CH, CH), F32),
        vmem((4, 1, COLS, CH), BF16),
        vmem((4, 2, 64, 128), BF16),
        vmem((4, 16, 128), F32),
        vmem((8, 64, 128), BF16),
        vmem((8, 16, 128), F32),
        *chunk,
        dma((6,)),
        dma((9,)),
        dma((9,)),
        dma((5, 10)),
        dma((5, 10)),
        dma((4, 2)),
        dma((4, 2)),
        dma((8,)),
        dma((8,)),
        pltpu.SemaphoreType.REGULAR((4,)),
        pltpu.SemaphoreType.REGULAR((3,)),
    ]
    g_in, sums = pl.pallas_call(
        kernel,
        out_shape=(jax.ShapeDtypeStruct(clip.shape, BF16), jax.ShapeDtypeStruct((128, 128), F32)),
        in_specs=[pl.BlockSpec(memory_space=pl.ANY)] * 4,
        out_specs=[pl.BlockSpec(memory_space=pl.ANY), pl.BlockSpec(memory_space=vmem)],
        scratch_shapes=scratch,
        compiler_params=pltpu.CompilerParams(collective_id=0, has_side_effects=True),
        name="block_backward",
    )(clip, weight, down, gout)
    g_in, g_conv, g_down = pl.pallas_call(
        hand_out,
        out_shape=(
            jax.ShapeDtypeStruct(clip.shape, BF16),
            jax.ShapeDtypeStruct((64, 108), F32),
            jax.ShapeDtypeStruct((12, 64), F32),
        ),
        in_specs=[pl.BlockSpec(memory_space=vmem)] * 2,
        out_specs=[pl.BlockSpec(memory_space=vmem)] * 3,
        name="hand_out",
    )(g_in, sums)
    return g_in, g_conv.T, g_down


def solution(mesh):
    placed = (P("tm", "height", None, None), P(), P(), P("tm", "height", None, None))
    return jax.shard_map(
        body,
        mesh=mesh,
        in_specs=placed,
        out_specs=(P("tm", "height", None, None), P("height", "tm"), P("height", "tm")),
        check_vma=False,
    )
```

```python
import jax
import jax.numpy as jnp
from jax import lax
from jax.experimental import pallas as pl
from jax.experimental.pallas import tpu as pltpu
from jax.sharding import PartitionSpec as P

MESH = pl.DeviceIdType.MESH
F32 = jnp.float32
BF16 = jnp.bfloat16
COLS = 128
CH = 256
SIZES = (112, 112, 112, 112, 64)
DOWN = 4
OWN_ROW = (1, 3, 3)
TAPS = ((0, 5, 2), (2, 4, 2), (3, 0, 1), (8, 0, 1))


def nt(lhs, rhs):
    return lax.dot_general(lhs, rhs, (((1,), (1,)), ((), ())), preferred_element_type=F32)


def nn(lhs, rhs):
    return jnp.dot(lhs, rhs, preferred_element_type=F32)


def sigmoid(value):
    return 1.0 / (1.0 + jnp.exp(-value))


def shifted(value, row):
    before = jnp.where(row == 0, 0.0, pltpu.roll(value, 1, 0))
    after = jnp.where(row == COLS - 1, 0.0, pltpu.roll(value, COLS - 1, 0))
    return before, after


def kernel(clip, weight, down, gout, g_in, sums, *scratch):
    scratch = list(scratch)
    take = lambda n: [scratch.pop(0) for _ in range(n)]
    (wgt, dwn, cl, go, acts, act_t, gs, cb, acc, part, part_d, held) = take(12)
    (zt, ztd, zr, zrd) = take(4)
    bufs = [take(9) for _ in SIZES]
    (loc_sem, halo_s, halo_r, red_s, red_r, zs, zsd, zrs, zrds, up, low) = take(11)

    tm = lax.axis_index("tm")
    h = lax.axis_index("height")
    core = lax.rem(tm, 2)
    yh = lax.div(tm, 2)
    x = lax.rem(h, 4)
    z = lax.rem(lax.div(h, 4), 8)
    yl = lax.div(h, 32)
    y = yh * 2 + yl

    def dev(xx, yy, zz, cc):
        return (lax.div(yy, 2) * 2 + cc, lax.rem(yy, 2) * 32 + zz * 4 + xx)

    def near(dt, dh):
        return (lax.rem(tm + dt + 4, 4), lax.rem(h + dh + 64, 64))

    def first(d):
        return dev(lax.rem(x + (1 - core) * d, 4), lax.rem(y + core * d, 4), z, core)

    def second(d):
        return dev(lax.rem(x + core * d, 4), lax.rem(y + (1 - core) * d, 4), z, core)

    def remote(src, dst, send, recv, device):
        return pltpu.make_async_remote_copy(
            src_ref=src, dst_ref=dst, send_sem=send, recv_sem=recv, device_id=device, device_id_type=MESH
        )

    barrier = pltpu.get_barrier_semaphore()
    ring = [first(d) for d in (1, 2, 3)] + [second(d) for d in (1, 2, 3)]
    ring += [dev(x, y, lax.rem(z + d, 8), core) for d in (1, 7)]
    for peer in ring:
        pl.semaphore_signal(barrier, inc=1, device_id=peer, device_id_type=MESH)
    has_h = {-1: lax.div(h + 62, 63), 0: 1, 1: lax.div(125 - h, 63)}
    has_t = {-1: lax.div(tm + 2, 3), 0: 1, 1: lax.div(5 - tm, 3)}
    expected = len(ring)
    for dt, dh in ((-1, 0), (1, 0), (0, -1), (0, 1), (-1, -1), (-1, 1), (1, -1), (1, 1)):
        there = has_t[dt] * has_h[dh]
        expected = expected + there

        @pl.when(there == 1)
        def _():
            pl.semaphore_signal(barrier, inc=1, device_id=near(dt, dh), device_id_type=MESH)

    loads = [
        pltpu.make_async_copy(clip.at[:, 0], cl.at[pl.ds(2, 4)], loc_sem.at[0]),
        pltpu.make_async_copy(gout.at[:, 0], go.at[1, pl.ds(0, 2)], loc_sem.at[1]),
        pltpu.make_async_copy(down, dwn, loc_sem.at[2]),
    ] + [pltpu.make_async_copy(weight.at[a], wgt.at[a], loc_sem.at[3 + a]) for a in range(3)]
    for load in loads:
        load.start()

    pl.semaphore_wait(barrier, expected)

    above, below = dev(x, y, lax.rem(z + 1, 8), core), dev(x, y, lax.rem(z + 7, 8), core)

    def tell(level):
        pl.semaphore_signal(up.at[level], inc=1, device_id=below, device_id_type=MESH)
        if level < 3:
            pl.semaphore_signal(low.at[level], inc=1, device_id=above, device_id_type=MESH)

    def hear(level):
        pl.semaphore_wait(up.at[level], 1)
        if level < 3:
            pl.semaphore_wait(low.at[level], 1)

    tell(0)

    halo = [
        (gout.at[:, 0], go.at[0, pl.ds(0, 2)], near(0, 1), h < 63, h > 0),
        (gout.at[:, 0], go.at[2, pl.ds(0, 2)], near(0, -1), h > 0, h < 63),
        (clip.at[pl.ds(2, 2), 0], cl.at[pl.ds(0, 2)], near(1, 0), tm < 3, tm > 0),
    ]
    odd, even = lax.rem(tm, 2) == 1, lax.rem(tm, 2) == 0
    for frame in range(2):
        late = gout.at[pl.ds(frame, 1), 0]
        place = pl.ds(2 + frame, 1)
        sends, takes = (tm > 0, tm < 3) if frame == 0 else (tm == 2, tm == 1)
        halo += [
            (late, go.at[1, place], near(-1, 0), tm > 0, tm < 3),
            (late, go.at[0, place], near(-1, 1), sends & (h < 63), takes & (h > 0)),
            (late, go.at[2, place], near(-1, -1), sends & (h > 0), takes & (h < 63)),
        ]
    halo += [
        (go.at[0, pl.ds(1, 1)], go.at[0, pl.ds(3, 1)], near(-1, 0), odd & (h > 0), even & (h > 0)),
        (go.at[2, pl.ds(1, 1)], go.at[2, pl.ds(3, 1)], near(-1, 0), odd & (h < 63), even & (h < 63)),
    ]
    copies = [remote(s, d, halo_s.at[i], halo_r.at[i], to) for i, (s, d, to, _, _) in enumerate(halo)]

    def when_start(i):
        @pl.when(halo[i][3])
        def _():
            copies[i].start()

    def when_recv(i):
        @pl.when(halo[i][4])
        def _():
            copies[i].wait_recv()

        @pl.when(jnp.logical_not(halo[i][4]))
        def _():
            dst = halo[i][1]
            dst[...] = jnp.zeros(dst.shape, BF16)

    def late_rows(r, there, direct, passed):
        for i in (direct, passed):
            @pl.when(halo[i][4])
            def _():
                copies[i].wait_recv()

        @pl.when(jnp.logical_not(there & (tm < 3)))
        def _():
            go[r, 3] = jnp.zeros((COLS, CH), BF16)

    for i in (3, 2, 4, 5, 0, 1):
        when_start(i)

    row = lax.broadcasted_iota(jnp.int32, (COLS, CH), 0)

    def act_frame(f, carry):
        value = cl[f].astype(F32)
        act = value * sigmoid(value)
        before, after = shifted(act, row)
        acts[0, f] = before.astype(BF16)
        acts[1, f] = act.astype(BF16)
        acts[2, f] = after.astype(BF16)
        act_t[f] = act.T.astype(BF16)
        return carry

    loads[0].wait()
    lax.fori_loop(2, 6, act_frame, 0)
    def conv_rows(b, carry):
        total = jnp.zeros((4 * COLS, CH), F32)
        for a in range(3):
            lhs = jnp.concatenate([acts[c, pl.ds(a, 4)].reshape(4 * COLS, CH) for c in range(3)], axis=1)
            total = total + nn(lhs, wgt[a, b].reshape(3 * CH, CH))
        own = cl[pl.ds(2, 4)].reshape(4 * COLS, CH).astype(F32)
        total = total + jnp.where(b == 1, own, 0.0)
        cb[b] = total.astype(BF16).reshape(4, COLS, CH)
        return carry

    def grad_rows(r):
        later = go[r, pl.ds(1, 2)].reshape(2 * COLS, CH)
        here = go[r, pl.ds(0, 2)].reshape(2 * COLS, CH)
        even = nt(later, dwn[0]) + nt(here, dwn[2])
        odd = nt(later, dwn[1])
        for v in range(2):
            place(r, 2 * v, even[v * COLS : (v + 1) * COLS])
            place(r, 2 * v + 1, odd[v * COLS : (v + 1) * COLS])

    def place(r, f, value):
        before, after = shifted(value, row)
        gs[0, r, f] = after.astype(BF16)
        gs[1, r, f] = value.astype(BF16)
        gs[2, r, f] = before.astype(BF16)

    def grad_tail():
        later = jnp.concatenate([go[r, 3] for r in range(3)], axis=0)
        here = jnp.concatenate([go[r, 2] for r in range(3)], axis=0)
        even = nt(later, dwn[0]) + nt(here, dwn[2])
        odd = nt(later, dwn[1])
        for r in range(3):
            place(r, 4, even[r * COLS : (r + 1) * COLS])
            place(r, 5, odd[r * COLS : (r + 1) * COLS])

    def down_terms():
        for k, pairs in ((0, ((0, 1), (2, 2))), (1, ((1, 1), (3, 2))), (2, ((0, 0), (2, 1)))):
            lhs = jnp.concatenate([cb[b, t] for b in range(3) for t, _ in pairs], axis=0)
            rhs = jnp.concatenate([go[2 - b, u] for b in range(3) for _, u in pairs], axis=0)
            part_d[k * CH : (k + 1) * CH, :] = lax.dot_general(
                lhs, rhs, (((0,), (0,)), ((), ())), preferred_element_type=F32
            )

    def taps(start, step, count):
        def one(i, carry):
            ab = start + step * i
            a, b = lax.div(ab, 3), lax.rem(ab, 3)
            lhs = jnp.concatenate([act_t[a + f] for f in range(4)], axis=1)
            for s in range(3):
                rhs = gs[s, 2 - b, pl.ds(0, 4)].reshape(4 * COLS, CH)
                part[pl.ds(pl.multiple_of((3 * ab + s) * CH, CH), CH), :] = nn(lhs, rhs)
            return carry

        lax.fori_loop(0, count, one, 0)

    def blocks(c, cc, put):
        def two(i, carry):
            l, pair = lax.div(i, 2), lax.rem(i, 2)
            if c == DOWN:
                for j in range(4):
                    base = pl.multiple_of(24 * (16 * l + 2 * (2 * j + cc) + pair), 8)
                    each(part_d, base, 16, 8, slice(16 * j, 16 * j + 16), l, pair)
            else:
                base = pl.multiple_of(216 * (16 * l + 2 * (2 * c + cc) + pair), 8)
                each(part, base, 112, 104, slice(0, 112), l, pair)
            return carry

        def each(src, base, size, skip, where, l, pair):
            for odd in range(2):
                value = src[pl.ds(base + skip * odd, size), :]
                xx = 2 * pair + odd
                for hi in range(2):
                    yy = 2 * hi + l
                    p = (1 - cc) * xx + cc * yy
                    q = (1 - cc) * yy + cc * xx
                    put(p, q, where, value[:, 128 * hi : 128 * hi + 128])

        lax.fori_loop(0, 4, two, 0)

    partner = dev(x, y, z, 1 - core)
    p0 = (1 - core) * x + core * y
    q0 = (1 - core) * y + core * x
    pn, pp, po = lax.rem(p0 + 1, 4), lax.rem(p0 + 3, 4), lax.rem(p0 + 2, 4)

    def message(c, i):
        s_, sr, b_, leg, dr, cs, cm, r_, rx = bufs[c]
        lo, hi = pl.ds(0, 2), pl.ds(2, 2)
        if i == 0:
            src, dst, to = s_, sr, partner
        elif i == 1:
            src, dst, to = b_.at[po, lo], leg.at[0], first(1)
        elif i == 2:
            src, dst, to = b_.at[po, hi], leg.at[1], first(3)
        elif i == 3:
            src, dst, to = b_.at[pn, hi], dr.at[0], first(1)
        elif i == 4:
            src, dst, to = b_.at[pp, lo], dr.at[1], first(3)
        elif i == 5:
            src, dst, to = cs.at[0], cm.at[0], first(1)
        elif i == 6:
            src, dst, to = cs.at[1], cm.at[1], first(3)
        else:
            d = i - 6
            src, dst, to = r_.at[lax.rem(q0 + d, 4)], rx.at[d - 1], second(d)
        return remote(src, dst, red_s.at[c, i], red_r.at[c, i], to)

    def hand_over(c):
        s_ = bufs[c][0]

        def put(p, q, where, value):
            s_[p, q, where] = value.astype(BF16)

        blocks(c, 1 - core, put)
        message(c, 0).start()

    def combine(c):
        sr, b_ = bufs[c][1], bufs[c][2]
        message(c, 0).wait_recv()

        def put(p, q, where, value):
            b_[p, q, where] = (value + sr[p, q, where].astype(F32)).astype(BF16)

        blocks(c, core, put)
        for i in (1, 2, 3, 4):
            message(c, i).start()

    def relay(c):
        _, _, b_, leg, _, cs, _, _, _ = bufs[c]
        message(c, 1).wait_recv()
        cs[0] = (b_[pn, pl.ds(0, 2)].astype(F32) + leg[0].astype(F32)).astype(BF16)
        message(c, 5).start()
        message(c, 2).wait_recv()
        cs[1] = (b_[pp, pl.ds(2, 2)].astype(F32) + leg[1].astype(F32)).astype(BF16)
        message(c, 6).start()

    def turn(c):
        _, _, b_, _, dr, _, cm, r_, _ = bufs[c]
        for i in (3, 4, 5, 6):
            message(c, i).wait_recv()
        for half in range(2):
            both = pl.ds(2 * half, 2)
            total = b_[p0, both].astype(F32) + cm[half].astype(F32) + dr[1 - half].astype(F32)
            r_[both] = total.astype(r_.dtype)
        for i in (7, 8, 9):
            message(c, i).start()

    lane = lax.broadcasted_iota(jnp.int32, (64, 128), 1)

    def z_send(src, dst, keep, send, recv, to_z, k):
        own = (to_z == z) & (core == k)

        @pl.when(own)
        def _():
            dst.at[z][...] = src[...]

        @pl.when(jnp.logical_not(own))
        def _():
            remote(src, dst.at[z], send, recv.at[z], dev(x, y, to_z, k)).start()

    def z_wait(src, dst, send, recv, to_z, k):
        @pl.when(jnp.logical_not((to_z == z) & (core == k)))
        def _():
            remote(src, dst.at[z], send, recv.at[z], dev(x, y, to_z, k)).wait_send()

    def leave(c):
        r_, rx = bufs[c][7], bufs[c][8]
        for i in (7, 8, 9):
            message(c, i).wait_recv()
        total = r_[q0].astype(F32)
        for d in range(3):
            total = total + rx[d].astype(F32)
        if c == DOWN:
            ztd[...] = total.reshape(4, 16, 128)
            for j in range(4):
                for k in range(2):
                    z_send(ztd.at[j], zrd, None, zsd.at[j, k], zrds, 2 * j + core, k)
        else:
            top, low = total[0:64], total[48:112]
            zt[c, 0] = jnp.where(lane < 64, top, pltpu.roll(low, 64, 1)).astype(BF16)
            zt[c, 1] = jnp.where(lane < 64, pltpu.roll(top, 64, 1), low).astype(BF16)
            for k in range(2):
                z_send(zt.at[c, k], zr, None, zs.at[c, k], zrs, 2 * c + core, k)

    def grad_act(b, total):
        for a in range(3):
            for s in range(3):
                total = total + nt(gs[s, 2 - b, pl.ds(2 - a, 4)].reshape(4 * COLS, CH), wgt[a, b, s])
        return total

    def finish(f, carry):
        value = cl[f + 2].astype(F32)
        sig = sigmoid(value)
        grad = acc[pl.ds(pl.multiple_of(f * COLS, COLS), COLS), :]
        g_in[f, 0] = (gs[1, 1, f].astype(F32) + grad * (sig * (1.0 + value * (1.0 - sig)))).astype(BF16)
        return carry

    for a in range(3):
        loads[3 + a].wait()

    def convolve():
        lax.fori_loop(0, 3, conv_rows, 0)

    def earlier():
        when_recv(2)
        lax.fori_loop(0, 2, act_frame, 0)

    @pl.when(tm != 2)
    def _():
        earlier()
        convolve()

    loads[1].wait()
    loads[2].wait()
    when_recv(3)
    grad_rows(1)

    @pl.when(tm == 2)
    def _():
        earlier()

    taps(*OWN_ROW)
    hear(0)
    tell(1)

    @pl.when(tm == 2)
    def _():
        convolve()

    for i in (0, 1, 4, 5):
        when_recv(i)
    for i in (6, 7, 8, 9, 10):
        when_start(i)
    grad_rows(0)
    grad_rows(2)
    taps(*TAPS[0])
    hand_over(0)
    taps(*TAPS[1])
    hand_over(1)
    combine(0)
    taps(*TAPS[2])
    hand_over(2)
    combine(1)
    taps(*TAPS[3])
    hand_over(3)
    down_terms()
    hand_over(DOWN)
    combine(2)
    combine(3)
    hear(1)
    tell(2)
    relay(0)
    combine(DOWN)
    relay(1)
    relay(2)
    relay(3)
    relay(DOWN)
    hear(2)
    tell(3)
    turn(0)
    turn(1)
    acc[...] = jnp.zeros(acc.shape, F32)
    when_recv(6)
    late_rows(0, h > 0, 7, 9)
    late_rows(2, h < 63, 8, 10)
    grad_tail()
    acc[...] = grad_act(0, acc[...])
    turn(2)
    turn(3)
    turn(DOWN)
    acc[...] = grad_act(1, acc[...])
    acc[...] = grad_act(2, acc[...])
    hear(3)
    leave(0)
    leave(1)
    leave(2)
    leave(3)
    leave(DOWN)
    lax.fori_loop(0, 4, finish, 0)

    mine = lax.rem(z, 2)
    for s in range(8):
        @pl.when(jnp.logical_not((z == s) & (core == mine)))
        def _():
            remote(ztd.at[0], zrd.at[s], zsd.at[0, 0], zrds.at[s], partner).wait_recv()
            remote(zt.at[0, 0], zr.at[s], zs.at[0, 0], zrs.at[s], partner).wait_recv()

    x_odd = lax.rem(x, 2) == 1
    total = zr[0].astype(F32)
    total_d = zrd[0].astype(F32)
    for s in range(1, 8):
        total = total + zr[s].astype(F32)
        total_d = total_d + zrd[s].astype(F32)
    whole = jnp.concatenate([total, pltpu.roll(total, 64, 1)[16:64]], axis=0)
    whole = jnp.where(x_odd, pltpu.roll(whole, 108, 0), whole)
    sums[0:112] = whole
    total_d = jnp.where(core == 1, pltpu.roll(total_d, 64, 1), total_d)
    total_d = jnp.where(x_odd, pltpu.roll(total_d, 12, 0), total_d)
    sums[112:128] = total_d

    for i in range(11):
        @pl.when(halo[i][3])
        def _():
            copies[i].wait_send()

    for c in range(5):
        for i in range(10):
            message(c, i).wait_send()
    for c in range(4):
        for k in range(2):
            z_wait(zt.at[c, k], zr, zs.at[c, k], zrs, 2 * c + core, k)
            z_wait(ztd.at[c], zrd, zsd.at[c, k], zrds, 2 * c + core, k)


def hand_out(given, sums, g_in, g_conv, g_down):
    g_in[...] = given[...]
    g_conv[...] = sums[0:112].T[0:64, 0:108]
    g_down[...] = sums[112:124, 0:64]


def body(clip, weight, down, gout):
    vmem = pltpu.VMEM
    chunk = []
    for n in SIZES:
        full, pair = (4, 4, n, 128), (2, 2, n, 128)
        chunk += [vmem(s, BF16) for s in (full, full, full, pair, pair, pair, pair)]
        later = BF16 if n == 112 else F32
        chunk += [vmem((4, n, 128), later), vmem((3, n, 128), later)]
    dma = pltpu.SemaphoreType.DMA
    scratch = [
        vmem((3, 3, 3, CH, CH), BF16),
        vmem((3, CH, CH), BF16),
        vmem((6, COLS, CH), BF16),
        vmem((3, 4, COLS, CH), BF16),
        vmem((3, 6, COLS, CH), BF16),
        vmem((6, CH, COLS), BF16),
        vmem((3, 3, 6, COLS, CH), BF16),
        vmem((3, 4, COLS, CH), BF16),
        vmem((4 * COLS, CH), F32),
        vmem((27 * CH, CH), F32),
        vmem((3 * CH, CH), F32),
        vmem((4, 1, COLS, CH), BF16),
        vmem((4, 2, 64, 128), BF16),
        vmem((4, 16, 128), F32),
        vmem((8, 64, 128), BF16),
        vmem((8, 16, 128), F32),
        *chunk,
        dma((6,)),
        dma((11,)),
        dma((11,)),
        dma((5, 10)),
        dma((5, 10)),
        dma((4, 2)),
        dma((4, 2)),
        dma((8,)),
        dma((8,)),
        pltpu.SemaphoreType.REGULAR((4,)),
        pltpu.SemaphoreType.REGULAR((3,)),
    ]
    g_in, sums = pl.pallas_call(
        kernel,
        out_shape=(vmem(clip.shape, BF16), vmem((128, 128), F32)),
        in_specs=[pl.BlockSpec(memory_space=pl.ANY)] * 4,
        out_specs=[pl.BlockSpec(memory_space=vmem), pl.BlockSpec(memory_space=vmem)],
        scratch_shapes=scratch,
        compiler_params=pltpu.CompilerParams(collective_id=0, has_side_effects=True),
        name="block_backward",
    )(clip, weight, down, gout)
    g_in, g_conv, g_down = pl.pallas_call(
        hand_out,
        out_shape=(
            jax.ShapeDtypeStruct(clip.shape, BF16),
            jax.ShapeDtypeStruct((64, 108), F32),
            jax.ShapeDtypeStruct((12, 64), F32),
        ),
        in_specs=[pl.BlockSpec(memory_space=vmem)] * 2,
        out_specs=[pl.BlockSpec(memory_space=vmem)] * 3,
        name="hand_out",
    )(pltpu.with_memory_space_constraint(g_in, vmem), pltpu.with_memory_space_constraint(sums, vmem))
    return g_in, g_conv.T, g_down


def solution(mesh):
    placed = (P("tm", "height", None, None), P(), P(), P("tm", "height", None, None))
    return jax.shard_map(
        body,
        mesh=mesh,
        in_specs=placed,
        out_specs=(P("tm", "height", None, None), P("height", "tm"), P("height", "tm")),
        check_vma=False,
    )
```

```python
import jax
import jax.numpy as jnp
from jax import lax
from jax.experimental import pallas as pl
from jax.experimental.pallas import tpu as pltpu
from jax.sharding import PartitionSpec as P

MESH = pl.DeviceIdType.MESH
F32 = jnp.float32
BF16 = jnp.bfloat16
COLS = 128
CH = 256
SIZES = (112, 112, 112, 112, 64)
DOWN = 4
OWN_ROW = (1, 3, 3)
ROW_ABOVE = (2, 3, 3)
TAPS = ((0, 0, 1), (6, 0, 1), (3, 0, 1))


def nt(lhs, rhs):
    return lax.dot_general(lhs, rhs, (((1,), (1,)), ((), ())), preferred_element_type=F32)


def nn(lhs, rhs):
    return jnp.dot(lhs, rhs, preferred_element_type=F32)


def sigmoid(value):
    return 1.0 / (1.0 + jnp.exp(-value))


def shifted(value, row):
    before = jnp.where(row == 0, 0.0, pltpu.roll(value, 1, 0))
    after = jnp.where(row == COLS - 1, 0.0, pltpu.roll(value, COLS - 1, 0))
    return before, after


def kernel(clip, weight, down, gout, g_in, sums, *scratch):
    scratch = list(scratch)
    take = lambda n: [scratch.pop(0) for _ in range(n)]
    (wgt, dwn, cl, go, acts, act_t, gs, cb, acc, part, part_d, held) = take(12)
    (zt, ztd, zr, zrd) = take(4)
    bufs = [take(9) for _ in SIZES]
    (loc_sem, halo_s, halo_r, red_s, red_r, zs, zsd, zrs, zrds, up, low) = take(11)

    tm = lax.axis_index("tm")
    h = lax.axis_index("height")
    core = lax.rem(tm, 2)
    yh = lax.div(tm, 2)
    x = lax.rem(h, 4)
    z = lax.rem(lax.div(h, 4), 8)
    yl = lax.div(h, 32)
    y = yh * 2 + yl

    def dev(xx, yy, zz, cc):
        return (lax.div(yy, 2) * 2 + cc, lax.rem(yy, 2) * 32 + zz * 4 + xx)

    def near(dt, dh):
        return (lax.rem(tm + dt + 4, 4), lax.rem(h + dh + 64, 64))

    def first(d):
        return dev(lax.rem(x + (1 - core) * d, 4), lax.rem(y + core * d, 4), z, core)

    def second(d):
        return dev(lax.rem(x + core * d, 4), lax.rem(y + (1 - core) * d, 4), z, core)

    def remote(src, dst, send, recv, device):
        return pltpu.make_async_remote_copy(
            src_ref=src, dst_ref=dst, send_sem=send, recv_sem=recv, device_id=device, device_id_type=MESH
        )

    barrier = pltpu.get_barrier_semaphore()
    ring = [first(d) for d in (1, 2, 3)] + [second(d) for d in (1, 2, 3)]
    ring += [dev(x, y, lax.rem(z + d, 8), core) for d in (1, 7)]
    for peer in ring:
        pl.semaphore_signal(barrier, inc=1, device_id=peer, device_id_type=MESH)
    has_h = {-1: lax.div(h + 62, 63), 0: 1, 1: lax.div(125 - h, 63)}
    has_t = {-1: lax.div(tm + 2, 3), 0: 1, 1: lax.div(5 - tm, 3)}
    expected = len(ring)
    for dt, dh in ((-1, 0), (1, 0), (0, -1), (0, 1), (-1, -1), (-1, 1), (1, -1), (1, 1)):
        there = has_t[dt] * has_h[dh]
        expected = expected + there

        @pl.when(there == 1)
        def _():
            pl.semaphore_signal(barrier, inc=1, device_id=near(dt, dh), device_id_type=MESH)

    loads = [
        pltpu.make_async_copy(clip.at[:, 0], cl.at[pl.ds(2, 4)], loc_sem.at[0]),
        pltpu.make_async_copy(gout.at[:, 0], go.at[1, pl.ds(0, 2)], loc_sem.at[1]),
        pltpu.make_async_copy(down, dwn, loc_sem.at[2]),
    ] + [pltpu.make_async_copy(weight.at[a], wgt.at[a], loc_sem.at[3 + a]) for a in range(3)]
    for load in loads:
        load.start()

    pl.semaphore_wait(barrier, expected)

    above, below = dev(x, y, lax.rem(z + 1, 8), core), dev(x, y, lax.rem(z + 7, 8), core)

    def tell(level):
        pl.semaphore_signal(up.at[level], inc=1, device_id=below, device_id_type=MESH)
        if level < 3:
            pl.semaphore_signal(low.at[level], inc=1, device_id=above, device_id_type=MESH)

    def hear(level):
        pl.semaphore_wait(up.at[level], 1)
        if level < 3:
            pl.semaphore_wait(low.at[level], 1)

    tell(0)

    halo = [
        (gout.at[:, 0], go.at[0, pl.ds(0, 2)], near(0, 1), h < 63, h > 0),
        (gout.at[:, 0], go.at[2, pl.ds(0, 2)], near(0, -1), h > 0, h < 63),
        (clip.at[pl.ds(2, 2), 0], cl.at[pl.ds(0, 2)], near(1, 0), tm < 3, tm > 0),
    ]
    odd, even = lax.rem(tm, 2) == 1, lax.rem(tm, 2) == 0
    for frame in range(2):
        late = gout.at[pl.ds(frame, 1), 0]
        place = pl.ds(2 + frame, 1)
        sends, takes = (tm > 0, tm < 3) if frame == 0 else (tm == 2, tm == 1)
        halo += [
            (late, go.at[1, place], near(-1, 0), tm > 0, tm < 3),
            (late, go.at[0, place], near(-1, 1), sends & (h < 63), takes & (h > 0)),
            (late, go.at[2, place], near(-1, -1), sends & (h > 0), takes & (h < 63)),
        ]
    halo += [
        (go.at[0, pl.ds(1, 1)], go.at[0, pl.ds(3, 1)], near(-1, 0), odd & (h > 0), even & (h > 0)),
        (go.at[2, pl.ds(1, 1)], go.at[2, pl.ds(3, 1)], near(-1, 0), odd & (h < 63), even & (h < 63)),
    ]
    copies = [remote(s, d, halo_s.at[i], halo_r.at[i], to) for i, (s, d, to, _, _) in enumerate(halo)]

    def when_start(i):
        @pl.when(halo[i][3])
        def _():
            copies[i].start()

    def when_recv(i):
        @pl.when(halo[i][4])
        def _():
            copies[i].wait_recv()

        @pl.when(jnp.logical_not(halo[i][4]))
        def _():
            dst = halo[i][1]
            dst[...] = jnp.zeros(dst.shape, BF16)

    def late_rows(r, there, direct, passed):
        for i in (direct, passed):
            @pl.when(halo[i][4])
            def _():
                copies[i].wait_recv()

        @pl.when(jnp.logical_not(there & (tm < 3)))
        def _():
            go[r, 3] = jnp.zeros((COLS, CH), BF16)

    for i in (3, 2, 4, 5, 0, 1):
        when_start(i)

    row = lax.broadcasted_iota(jnp.int32, (COLS, CH), 0)

    def act_frame(f, carry):
        value = cl[f].astype(F32)
        act = value * sigmoid(value)
        before, after = shifted(act, row)
        acts[0, f] = before.astype(BF16)
        acts[1, f] = act.astype(BF16)
        acts[2, f] = after.astype(BF16)
        act_t[f] = act.T.astype(BF16)
        return carry

    loads[0].wait()
    lax.fori_loop(2, 6, act_frame, 0)
    def conv_rows(b, carry):
        total = jnp.zeros((4 * COLS, CH), F32)
        for a in range(3):
            lhs = jnp.concatenate([acts[c, pl.ds(a, 4)].reshape(4 * COLS, CH) for c in range(3)], axis=1)
            total = total + nn(lhs, wgt[a, b].reshape(3 * CH, CH))
        own = cl[pl.ds(2, 4)].reshape(4 * COLS, CH).astype(F32)
        total = total + jnp.where(b == 1, own, 0.0)
        cb[b] = total.astype(BF16).reshape(4, COLS, CH)
        return carry

    def grad_rows(r):
        later = go[r, pl.ds(1, 2)].reshape(2 * COLS, CH)
        here = go[r, pl.ds(0, 2)].reshape(2 * COLS, CH)
        even = nt(later, dwn[0]) + nt(here, dwn[2])
        odd = nt(later, dwn[1])
        for v in range(2):
            place(r, 2 * v, even[v * COLS : (v + 1) * COLS])
            place(r, 2 * v + 1, odd[v * COLS : (v + 1) * COLS])

    def place(r, f, value):
        before, after = shifted(value, row)
        gs[0, r, f] = after.astype(BF16)
        gs[1, r, f] = value.astype(BF16)
        gs[2, r, f] = before.astype(BF16)

    def grad_tail():
        later = jnp.concatenate([go[r, 3] for r in range(3)], axis=0)
        here = jnp.concatenate([go[r, 2] for r in range(3)], axis=0)
        even = nt(later, dwn[0]) + nt(here, dwn[2])
        odd = nt(later, dwn[1])
        for r in range(3):
            place(r, 4, even[r * COLS : (r + 1) * COLS])
            place(r, 5, odd[r * COLS : (r + 1) * COLS])

    def down_terms():
        for k, pairs in ((0, ((0, 1), (2, 2))), (1, ((1, 1), (3, 2))), (2, ((0, 0), (2, 1)))):
            lhs = jnp.concatenate([cb[b, t] for b in range(3) for t, _ in pairs], axis=0)
            rhs = jnp.concatenate([go[2 - b, u] for b in range(3) for _, u in pairs], axis=0)
            part_d[k * CH : (k + 1) * CH, :] = lax.dot_general(
                lhs, rhs, (((0,), (0,)), ((), ())), preferred_element_type=F32
            )

    def taps(start, step, count):
        def one(i, carry):
            ab = start + step * i
            a, b = lax.div(ab, 3), lax.rem(ab, 3)
            lhs = jnp.concatenate([act_t[a + f] for f in range(4)], axis=1)
            for s in range(3):
                rhs = gs[s, 2 - b, pl.ds(0, 4)].reshape(4 * COLS, CH)
                part[pl.ds(pl.multiple_of((3 * ab + s) * CH, CH), CH), :] = nn(lhs, rhs)
            return carry

        lax.fori_loop(0, count, one, 0)

    def blocks(c, cc, put):
        def two(i, carry):
            l, pair = lax.div(i, 2), lax.rem(i, 2)
            if c == DOWN:
                for j in range(4):
                    base = pl.multiple_of(24 * (16 * l + 2 * (2 * j + cc) + pair), 8)
                    each(part_d, base, 16, 8, slice(16 * j, 16 * j + 16), l, pair)
            else:
                base = pl.multiple_of(216 * (16 * l + 2 * (2 * c + cc) + pair), 8)
                each(part, base, 112, 104, slice(0, 112), l, pair)
            return carry

        def each(src, base, size, skip, where, l, pair):
            for odd in range(2):
                value = src[pl.ds(base + skip * odd, size), :]
                xx = 2 * pair + odd
                for hi in range(2):
                    yy = 2 * hi + l
                    p = (1 - cc) * xx + cc * yy
                    q = (1 - cc) * yy + cc * xx
                    put(p, q, where, value[:, 128 * hi : 128 * hi + 128])

        lax.fori_loop(0, 4, two, 0)

    partner = dev(x, y, z, 1 - core)
    p0 = (1 - core) * x + core * y
    q0 = (1 - core) * y + core * x
    pn, pp, po = lax.rem(p0 + 1, 4), lax.rem(p0 + 3, 4), lax.rem(p0 + 2, 4)

    def message(c, i):
        s_, sr, b_, leg, dr, cs, cm, r_, rx = bufs[c]
        lo, hi = pl.ds(0, 2), pl.ds(2, 2)
        if i == 0:
            src, dst, to = s_, sr, partner
        elif i == 1:
            src, dst, to = b_.at[po, lo], leg.at[0], first(1)
        elif i == 2:
            src, dst, to = b_.at[po, hi], leg.at[1], first(3)
        elif i == 3:
            src, dst, to = b_.at[pn, hi], dr.at[0], first(1)
        elif i == 4:
            src, dst, to = b_.at[pp, lo], dr.at[1], first(3)
        elif i == 5:
            src, dst, to = cs.at[0], cm.at[0], first(1)
        elif i == 6:
            src, dst, to = cs.at[1], cm.at[1], first(3)
        else:
            d = i - 6
            src, dst, to = r_.at[lax.rem(q0 + d, 4)], rx.at[d - 1], second(d)
        return remote(src, dst, red_s.at[c, i], red_r.at[c, i], to)

    def hand_over(c):
        s_ = bufs[c][0]

        def put(p, q, where, value):
            s_[p, q, where] = value.astype(BF16)

        blocks(c, 1 - core, put)
        message(c, 0).start()

    def combine(c):
        sr, b_ = bufs[c][1], bufs[c][2]
        message(c, 0).wait_recv()

        def put(p, q, where, value):
            b_[p, q, where] = (value + sr[p, q, where].astype(F32)).astype(BF16)

        blocks(c, core, put)
        for i in (1, 2, 3, 4):
            message(c, i).start()

    def relay(c):
        _, _, b_, leg, _, cs, _, _, _ = bufs[c]
        message(c, 1).wait_recv()
        cs[0] = (b_[pn, pl.ds(0, 2)].astype(F32) + leg[0].astype(F32)).astype(BF16)
        message(c, 5).start()
        message(c, 2).wait_recv()
        cs[1] = (b_[pp, pl.ds(2, 2)].astype(F32) + leg[1].astype(F32)).astype(BF16)
        message(c, 6).start()

    def turn(c):
        _, _, b_, _, dr, _, cm, r_, _ = bufs[c]
        for i in (3, 4, 5, 6):
            message(c, i).wait_recv()
        for half in range(2):
            both = pl.ds(2 * half, 2)
            total = b_[p0, both].astype(F32) + cm[half].astype(F32) + dr[1 - half].astype(F32)
            r_[both] = total.astype(r_.dtype)
        for i in (7, 8, 9):
            message(c, i).start()

    lane = lax.broadcasted_iota(jnp.int32, (64, 128), 1)

    def z_send(src, dst, keep, send, recv, to_z, k):
        own = (to_z == z) & (core == k)

        @pl.when(own)
        def _():
            dst.at[z][...] = src[...]

        @pl.when(jnp.logical_not(own))
        def _():
            remote(src, dst.at[z], send, recv.at[z], dev(x, y, to_z, k)).start()

    def z_wait(src, dst, send, recv, to_z, k):
        @pl.when(jnp.logical_not((to_z == z) & (core == k)))
        def _():
            remote(src, dst.at[z], send, recv.at[z], dev(x, y, to_z, k)).wait_send()

    def leave(c):
        r_, rx = bufs[c][7], bufs[c][8]
        for i in (7, 8, 9):
            message(c, i).wait_recv()
        total = r_[q0].astype(F32)
        for d in range(3):
            total = total + rx[d].astype(F32)
        if c == DOWN:
            ztd[...] = total.reshape(4, 16, 128)
            for j in range(4):
                for k in range(2):
                    z_send(ztd.at[j], zrd, None, zsd.at[j, k], zrds, 2 * j + core, k)
        else:
            top, low = total[0:64], total[48:112]
            zt[c, 0] = jnp.where(lane < 64, top, pltpu.roll(low, 64, 1)).astype(BF16)
            zt[c, 1] = jnp.where(lane < 64, pltpu.roll(top, 64, 1), low).astype(BF16)
            for k in range(2):
                z_send(zt.at[c, k], zr, None, zs.at[c, k], zrs, 2 * c + core, k)

    def grad_act(b, total):
        for a in range(3):
            for s in range(3):
                total = total + nt(gs[s, 2 - b, pl.ds(2 - a, 4)].reshape(4 * COLS, CH), wgt[a, b, s])
        return total

    def finish(f, carry):
        value = cl[f + 2].astype(F32)
        sig = sigmoid(value)
        grad = acc[pl.ds(pl.multiple_of(f * COLS, COLS), COLS), :]
        g_in[f, 0] = (gs[1, 1, f].astype(F32) + grad * (sig * (1.0 + value * (1.0 - sig)))).astype(BF16)
        return carry

    for a in range(3):
        loads[3 + a].wait()

    def convolve():
        lax.fori_loop(0, 3, conv_rows, 0)

    def earlier():
        when_recv(2)
        lax.fori_loop(0, 2, act_frame, 0)

    @pl.when(tm != 2)
    def _():
        earlier()
        convolve()

    loads[1].wait()
    loads[2].wait()
    when_recv(3)
    grad_rows(1)

    @pl.when(tm == 2)
    def _():
        earlier()

    taps(*OWN_ROW)
    hear(0)
    tell(1)

    @pl.when(tm == 2)
    def _():
        convolve()

    for i in (0, 4):
        when_recv(i)
    grad_rows(0)
    taps(*ROW_ABOVE)
    for i in (1, 5):
        when_recv(i)
    for i in (6, 7, 8, 9, 10):
        when_start(i)
    grad_rows(2)
    taps(*TAPS[0])
    hand_over(0)
    taps(*TAPS[1])
    hand_over(1)
    combine(0)
    taps(*TAPS[2])
    hand_over(2)
    combine(1)
    hand_over(3)
    down_terms()
    hand_over(DOWN)
    combine(2)
    combine(3)
    hear(1)
    tell(2)
    relay(0)
    combine(DOWN)
    relay(1)
    relay(2)
    relay(3)
    relay(DOWN)
    hear(2)
    tell(3)
    turn(0)
    turn(1)
    acc[...] = jnp.zeros(acc.shape, F32)
    when_recv(6)
    late_rows(0, h > 0, 7, 9)
    late_rows(2, h < 63, 8, 10)
    grad_tail()
    acc[...] = grad_act(0, acc[...])
    turn(2)
    turn(3)
    turn(DOWN)
    acc[...] = grad_act(1, acc[...])
    acc[...] = grad_act(2, acc[...])
    hear(3)
    leave(0)
    leave(1)
    leave(2)
    leave(3)
    leave(DOWN)
    lax.fori_loop(0, 4, finish, 0)

    mine = lax.rem(z, 2)
    for s in range(8):
        @pl.when(jnp.logical_not((z == s) & (core == mine)))
        def _():
            remote(ztd.at[0], zrd.at[s], zsd.at[0, 0], zrds.at[s], partner).wait_recv()
            remote(zt.at[0, 0], zr.at[s], zs.at[0, 0], zrs.at[s], partner).wait_recv()

    x_odd = lax.rem(x, 2) == 1
    total = zr[0].astype(F32)
    total_d = zrd[0].astype(F32)
    for s in range(1, 8):
        total = total + zr[s].astype(F32)
        total_d = total_d + zrd[s].astype(F32)
    whole = jnp.concatenate([total, pltpu.roll(total, 64, 1)[16:64]], axis=0)
    whole = jnp.where(x_odd, pltpu.roll(whole, 108, 0), whole)
    sums[0:112] = whole
    total_d = jnp.where(core == 1, pltpu.roll(total_d, 64, 1), total_d)
    total_d = jnp.where(x_odd, pltpu.roll(total_d, 12, 0), total_d)
    sums[112:128] = total_d

    for i in range(11):
        @pl.when(halo[i][3])
        def _():
            copies[i].wait_send()

    for c in range(5):
        for i in range(10):
            message(c, i).wait_send()
    for c in range(4):
        for k in range(2):
            z_wait(zt.at[c, k], zr, zs.at[c, k], zrs, 2 * c + core, k)
            z_wait(ztd.at[c], zrd, zsd.at[c, k], zrds, 2 * c + core, k)


def hand_out(given, sums, g_in, g_conv, g_down):
    g_in[...] = given[...]
    g_conv[...] = sums[0:112].T[0:64, 0:108]
    g_down[...] = sums[112:124, 0:64]


def body(clip, weight, down, gout):
    vmem = pltpu.VMEM
    chunk = []
    for n in SIZES:
        full, pair = (4, 4, n, 128), (2, 2, n, 128)
        chunk += [vmem(s, BF16) for s in (full, full, full, pair, pair, pair, pair)]
        later = BF16 if n == 112 else F32
        chunk += [vmem((4, n, 128), later), vmem((3, n, 128), later)]
    dma = pltpu.SemaphoreType.DMA
    scratch = [
        vmem((3, 3, 3, CH, CH), BF16),
        vmem((3, CH, CH), BF16),
        vmem((6, COLS, CH), BF16),
        vmem((3, 4, COLS, CH), BF16),
        vmem((3, 6, COLS, CH), BF16),
        vmem((6, CH, COLS), BF16),
        vmem((3, 3, 6, COLS, CH), BF16),
        vmem((3, 4, COLS, CH), BF16),
        vmem((4 * COLS, CH), F32),
        vmem((27 * CH, CH), F32),
        vmem((3 * CH, CH), F32),
        vmem((4, 1, COLS, CH), BF16),
        vmem((4, 2, 64, 128), BF16),
        vmem((4, 16, 128), F32),
        vmem((8, 64, 128), BF16),
        vmem((8, 16, 128), F32),
        *chunk,
        dma((6,)),
        dma((11,)),
        dma((11,)),
        dma((5, 10)),
        dma((5, 10)),
        dma((4, 2)),
        dma((4, 2)),
        dma((8,)),
        dma((8,)),
        pltpu.SemaphoreType.REGULAR((4,)),
        pltpu.SemaphoreType.REGULAR((3,)),
    ]
    g_in, sums = pl.pallas_call(
        kernel,
        out_shape=(vmem(clip.shape, BF16), vmem((128, 128), F32)),
        in_specs=[pl.BlockSpec(memory_space=pl.ANY)] * 4,
        out_specs=[pl.BlockSpec(memory_space=vmem), pl.BlockSpec(memory_space=vmem)],
        scratch_shapes=scratch,
        compiler_params=pltpu.CompilerParams(collective_id=0, has_side_effects=True),
        name="block_backward",
    )(clip, weight, down, gout)
    g_in, g_conv, g_down = pl.pallas_call(
        hand_out,
        out_shape=(
            jax.ShapeDtypeStruct(clip.shape, BF16),
            jax.ShapeDtypeStruct((64, 108), F32),
            jax.ShapeDtypeStruct((12, 64), F32),
        ),
        in_specs=[pl.BlockSpec(memory_space=vmem)] * 2,
        out_specs=[pl.BlockSpec(memory_space=vmem)] * 3,
        name="hand_out",
    )(pltpu.with_memory_space_constraint(g_in, vmem), pltpu.with_memory_space_constraint(sums, vmem))
    return g_in, g_conv.T, g_down


def solution(mesh):
    placed = (P("tm", "height", None, None), P(), P(), P("tm", "height", None, None))
    return jax.shard_map(
        body,
        mesh=mesh,
        in_specs=placed,
        out_specs=(P("tm", "height", None, None), P("height", "tm"), P("height", "tm")),
        check_vma=False,
    )
```
